128 devices in a mesh: facet: 16 (over x, z_lo, core), col: 8 (over z_hi, y).
Axes of the slice: x: 4, y: 4, z: 4 (z_hi: 2, z_lo: 2; z = z_hi * 2 + z_lo), core: 2. Of those that a mesh axis runs over, the one named last changes fastest.
Arguments:
- strips: float32 [16, 2, 384, 2048], P('facet', None, 'col'), may hold values from -6 to 6
- sub_offset: int32 [8, 16], replicated, may hold values from 0 to 2047
- uv_cells: int32 [8, 16, 2, 128], P('col', 'facet'), may hold values from 0 to 255
- measured: float32 [8, 16, 2, 128], P('col', 'facet'), may hold values from -6 to 6
Outputs:
- dirty_image: float32 [16, 2, 384, 2048], P('facet', None, 'col')
- residual_vis: float32 [8, 16, 2, 128], P('col', 'facet')
The draws below stay inside these ranges and needn't reach their ends.
All inputs are finite; a program needn't handle non-finite values.
Results may differ from the reference program's by a relative error of at most 0.0003.
Values sent between devices are 32-bit elements; how exact they have to be, the bound alone decides.
No kernel may reach another device: no remote copies, remote signals or barrier semaphores. Data moves between devices by JAX's collectives and lax.ppermute only.
A program may use at most 64 MiB of HBM per device.

```python
import math
import jax
import jax.numpy as jnp
from jax import lax

CONTRIB_WIDTH = 48
FACET_STRIP_LEN = 2048
SUBGRID_SIZE = 256
VIS_PER_SUBGRID = 128
FACETS = 16
COLS = 8
FR = 384
SG_COL = 16
SUBGRID_TOTAL = 128
N_FACET = 16


def with_ends(entries, stream_key, low, high):
    spot = [jax.random.randint(jax.random.fold_in(stream_key, axis), (), 0, length) for axis, length in enumerate(entries.shape)]
    longest = entries.shape.index(max(entries.shape))
    beside = spot[:longest] + [(spot[longest] + 1) % entries.shape[longest]] + spot[longest + 1:]
    return entries.at[tuple(spot)].set(low).at[tuple(beside)].set(high)


def level_of(own_key, dims, shards, low, largest):
    gain, own = 1.0, jax.random.fold_in(own_key, 6)
    for position, parts in shards:
        steps = jnp.exp(jax.random.uniform(jax.random.fold_in(own, position), (parts,), jnp.float32, low / len(shards), largest / len(shards)))
        gain = gain * jnp.repeat(steps, dims[position] // parts).reshape([-1 if axis == position else 1 for axis in range(len(dims))])
    return gain


def bell_draw(rng, dims, deviation, bound, shards=(), held_as=jnp.bfloat16):
    loudness = level_of(rng, dims, shards, -0.22, 0.18) if shards else 1.0
    entries = jax.random.normal(rng, dims, jnp.float32) * deviation * loudness
    return jnp.minimum(jnp.maximum(entries, -bound), bound).astype(held_as)


def setup_inputs(seed: int = 0) -> dict:
    splits = jax.random.split(jax.random.key(seed), 5)
    strips = bell_draw(splits[0], (FACETS, 2, FR, FACET_STRIP_LEN), 1.0, 6.0, ((0, 16), (2, 8)), jnp.float32)
    sub_offset = with_ends(jax.random.randint(splits[1], (COLS, SG_COL), 0, FACET_STRIP_LEN), jax.random.fold_in(splits[1], 1), 0, FACET_STRIP_LEN - 1).astype(jnp.int32)
    uv_cells = with_ends(jax.random.randint(splits[2], (COLS, SG_COL, 2, VIS_PER_SUBGRID), 0, SUBGRID_SIZE), jax.random.fold_in(splits[2], 1), 0, SUBGRID_SIZE - 1).astype(jnp.int32)
    measured = bell_draw(splits[3], (COLS, SG_COL, 2, VIS_PER_SUBGRID), 1.0, 6.0, ((0, 8), (1, 16)), jnp.float32)
    return dict(strips=strips, sub_offset=sub_offset, uv_cells=uv_cells, measured=measured)


def complex_product(ar, ai, br, bi):
    high_precision = lax.Precision.HIGHEST
    rr = jnp.dot(ar, br, precision=high_precision, preferred_element_type=jnp.float32) - jnp.dot(ai, bi, precision=high_precision, preferred_element_type=jnp.float32)
    ri = jnp.dot(ar, bi, precision=high_precision, preferred_element_type=jnp.float32) + jnp.dot(ai, br, precision=high_precision, preferred_element_type=jnp.float32)
    return (rr, ri)

def phase_terms(numer, denom):
    angle = (numer % denom).astype(jnp.float32) * (2.0 * math.pi / denom)
    return (jnp.cos(angle), jnp.sin(angle))

def facet_strip_kernel(grid_offset, strip_width, strip_length):
    rows = jnp.arange(strip_length, dtype=jnp.int32)[:, None]
    cols = jnp.arange(strip_width, dtype=jnp.int32)[None, :]
    cosine, sine = phase_terms(rows * (grid_offset + cols), strip_length)
    norm = 1.0 / math.sqrt(strip_length)
    return (cosine * norm, -sine * norm)

def einsum_hi(form, left, right):
    return jnp.einsum(form, left, right, precision=lax.Precision.HIGHEST)

def subgrid_update(kernel_real, kernel_imaginary, u_coordinates, v_coordinates, measured_real, measured_imaginary, facet_count):
    strip_width = kernel_real.shape[-1]
    total = strip_width * facet_count
    factor = (facet_count * strip_width * strip_width) ** (-0.25)
    grid_cells = jnp.arange(SUBGRID_SIZE, dtype=jnp.int32)
    cosine, sine = phase_terms(grid_cells[:, None] * jnp.arange(total, dtype=jnp.int32)[None, :], total)
    ere = factor * cosine
    eim = factor * sine
    ebre = ere.reshape(SUBGRID_SIZE, facet_count, strip_width)
    ebim = eim.reshape(SUBGRID_SIZE, facet_count, strip_width)
    are = einsum_hi('ufk,fkl->ufl', ebre, kernel_real) - einsum_hi('ufk,fkl->ufl', ebim, kernel_imaginary)
    aim = einsum_hi('ufk,fkl->ufl', ebre, kernel_imaginary) + einsum_hi('ufk,fkl->ufl', ebim, kernel_real)
    sre, sim = complex_product(are.reshape(SUBGRID_SIZE, total), aim.reshape(SUBGRID_SIZE, total), ere.T, eim.T)
    ucos, usin = phase_terms(u_coordinates[:, None] * grid_cells[None, :], SUBGRID_SIZE)
    v_cosine, v_sine = phase_terms(v_coordinates[:, None] * grid_cells[None, :], SUBGRID_SIZE)
    fure, fuim = (ucos, -usin)
    fvre, fvim = (v_cosine, -v_sine)
    tre, tim = complex_product(fure, fuim, sre, sim)
    pred_re = lax.optimization_barrier(jnp.sum(tre * fvre - tim * fvim, axis=1)) / SUBGRID_SIZE
    pred_im = lax.optimization_barrier(jnp.sum(tre * fvim + tim * fvre, axis=1)) / SUBGRID_SIZE
    residual_real = measured_real - pred_re
    residual_imaginary = measured_imaginary - pred_im
    gre = fvre * residual_real[:, None] + fvim * residual_imaginary[:, None]
    gim = fvre * residual_imaginary[:, None] - fvim * residual_real[:, None]
    spre, spim = complex_product(fure.T, -fuim.T, gre, gim)
    bre, bim = complex_product(ere.T, -eim.T, spre, spim)
    bre = bre.reshape(facet_count, strip_width, SUBGRID_SIZE)
    bim = bim.reshape(facet_count, strip_width, SUBGRID_SIZE)
    kernel_phase_real = einsum_hi('fka,afl->fkl', bre, ebre) + einsum_hi('fka,afl->fkl', bim, ebim)
    kernel_phase_imaginary = einsum_hi('fka,afl->fkl', bim, ebre) - einsum_hi('fka,afl->fkl', bre, ebim)
    return (residual_real, residual_imaginary, kernel_phase_real, kernel_phase_imaginary)

def reference(strips, sub_offset, uv_cells, measured):
    facet_count = N_FACET
    flattened_offsets = sub_offset.reshape(SUBGRID_TOTAL)
    flattened_uv_cells = uv_cells.reshape(SUBGRID_TOTAL, 2, VIS_PER_SUBGRID)
    flattened_measured = measured.reshape(SUBGRID_TOTAL, 2, VIS_PER_SUBGRID)

    def single_subgrid(input_arrays):
        subgrid_index, grid_offset, uv_points, measured_vis = input_arrays
        column = (subgrid_index // SG_COL).astype(jnp.int32)
        block_slice = lax.dynamic_slice_in_dim(strips, (column * CONTRIB_WIDTH).astype(jnp.int32), CONTRIB_WIDTH, 2)
        vis_real, vis_imaginary = facet_strip_kernel(grid_offset, CONTRIB_WIDTH, FACET_STRIP_LEN)
        kernel_real, kernel_imaginary = complex_product(block_slice[:, 0].reshape(facet_count * CONTRIB_WIDTH, FACET_STRIP_LEN), block_slice[:, 1].reshape(facet_count * CONTRIB_WIDTH, FACET_STRIP_LEN), vis_real, vis_imaginary)
        residual_real, residual_imaginary, kernel_phase_real, kernel_phase_imaginary = subgrid_update(kernel_real.reshape(facet_count, CONTRIB_WIDTH, CONTRIB_WIDTH), kernel_imaginary.reshape(facet_count, CONTRIB_WIDTH, CONTRIB_WIDTH), uv_points[0], uv_points[1], measured_vis[0], measured_vis[1], facet_count)
        return (jnp.stack([residual_real, residual_imaginary]), jnp.stack([kernel_phase_real, kernel_phase_imaginary], axis=1))
    residual_output, back_projection = lax.map(single_subgrid, (jnp.arange(SUBGRID_TOTAL, dtype=jnp.int32), flattened_offsets, flattened_uv_cells, flattened_measured))
    residual_vis = residual_output.reshape(COLS, SG_COL, 2, VIS_PER_SUBGRID)
    back_projection = back_projection.reshape(COLS, SG_COL, facet_count, 2, CONTRIB_WIDTH, CONTRIB_WIDTH)
    high_precision = lax.Precision.HIGHEST

    def column_step(carry, input_arrays):
        col, offsets, returned = input_arrays

        def add_item(acc, item):
            grid_offset, piece = item
            vis_real, vis_imaginary = facet_strip_kernel(grid_offset, CONTRIB_WIDTH, FACET_STRIP_LEN)
            phase_real = piece[:, 0].reshape(facet_count * CONTRIB_WIDTH, CONTRIB_WIDTH)
            phase_imaginary = piece[:, 1].reshape(facet_count * CONTRIB_WIDTH, CONTRIB_WIDTH)
            right_real = jnp.dot(phase_real, vis_real.T, precision=high_precision, preferred_element_type=jnp.float32) + jnp.dot(phase_imaginary, vis_imaginary.T, precision=high_precision, preferred_element_type=jnp.float32)
            right_imaginary = jnp.dot(phase_imaginary, vis_real.T, precision=high_precision, preferred_element_type=jnp.float32) - jnp.dot(phase_real, vis_imaginary.T, precision=high_precision, preferred_element_type=jnp.float32)
            return ((acc[0] + right_real, acc[1] + right_imaginary), None)
        zero = jnp.zeros((facet_count * CONTRIB_WIDTH, FACET_STRIP_LEN), jnp.float32)
        (right_real, right_imaginary), _ = lax.scan(add_item, (zero, zero), (offsets, returned))
        right_real = right_real.reshape(facet_count, CONTRIB_WIDTH, FACET_STRIP_LEN)
        right_imaginary = right_imaginary.reshape(facet_count, CONTRIB_WIDTH, FACET_STRIP_LEN)
        rows = jnp.arange(FR, dtype=jnp.int32)[:, None]
        keys = jnp.arange(CONTRIB_WIDTH, dtype=jnp.int32)[None, :] + CONTRIB_WIDTH * col
        cosine, sine = phase_terms(rows * keys, FR)
        phase_real = cosine / math.sqrt(FR)
        phase_imaginary = sine / math.sqrt(FR)
        dre = einsum_hi('rk,fkw->frw', phase_real, right_real) - einsum_hi('rk,fkw->frw', phase_imaginary, right_imaginary)
        dim = einsum_hi('rk,fkw->frw', phase_real, right_imaginary) + einsum_hi('rk,fkw->frw', phase_imaginary, right_real)
        return ((carry[0] + dre, carry[1] + dim), None)
    start = jnp.zeros((facet_count, FR, FACET_STRIP_LEN), jnp.float32)
    (dre, dim), _ = lax.scan(column_step, (start, start), (jnp.arange(COLS, dtype=jnp.int32), sub_offset, back_projection))
    dirty_image = jnp.stack([dre, dim], axis=1)
    return (dirty_image, residual_vis)
```

```python
import math

import jax
import jax.numpy as jnp
import ml_dtypes
import numpy as np
from jax import lax
from jax.experimental import pallas as pl
from jax.experimental.pallas import tpu as pltpu
from jax.sharding import PartitionSpec as P

SUBGRID = 256
WIDTH = 48
LENGTH = 2048
FACETS = 16
COLS = 8
ROWS = 384
PADDED = LENGTH + WIDTH
TOTAL = FACETS * WIDTH
F32 = jnp.float32
BF16 = jnp.bfloat16


def split_np(x):
    x = np.asarray(x, np.float32)
    hi = x.astype(ml_dtypes.bfloat16)
    lo = (x - hi.astype(np.float32)).astype(ml_dtypes.bfloat16)
    return hi, lo


def split(x):
    hi = x.astype(BF16)
    lo = (x - hi.astype(F32)).astype(BF16)
    return hi, lo


def dot(a, b, transposed=False):
    dims = (((1,), (1 if transposed else 0,)), ((), ()))
    return lax.dot_general(a, b, dims, preferred_element_type=F32)


def dot3(a, b, transposed=False):
    (ah, al), (bh, bl) = a, b
    return dot(ah, bh, transposed) + dot(ah, bl, transposed) + dot(al, bh, transposed)


def fft_list(xs, sign):
    n = len(xs)
    if n == 1:
        return xs
    even = fft_list(xs[0::2], sign)
    odd = fft_list(xs[1::2], sign)
    half = n // 2
    out = [None] * n
    for k in range(half):
        (er, ei), (r, i) = even[k], odd[k]
        if k == 0:
            tr, ti = r, i
        elif 4 * k == n:
            tr, ti = -sign * i, sign * r
        elif 8 * k == n:
            h = math.sqrt(0.5)
            tr, ti = h * (r - sign * i), h * (i + sign * r)
        elif 8 * k == 3 * n:
            h = math.sqrt(0.5)
            tr, ti = -h * (r + sign * i), h * (sign * r - i)
        else:
            c = math.cos(2 * math.pi * k / n)
            s = sign * math.sin(2 * math.pi * k / n)
            tr, ti = c * r - s * i, s * r + c * i
        out[k] = (er + tr, ei + ti)
        out[k + half] = (er - tr, ei - ti)
    return out


def tables():
    lane = np.arange(128)
    beta = np.arange(16)[:, None]
    ang = 2 * np.pi * ((lane[None, :] * beta) % LENGTH) / LENGTH
    norm = 1 / math.sqrt(LENGTH)
    twiddle = (np.stack([np.cos(ang), np.sin(ang)]) * norm).astype(np.float32)
    ang = 2 * np.pi * ((lane[:, None] * lane[None, :]) % 128) / 128
    cos, sin = np.cos(ang), np.sin(ang)
    forward = np.stack(split_np(np.concatenate([cos, sin], axis=1)))
    backward = np.stack(
        split_np(
            np.concatenate(
                [np.concatenate([cos, sin], axis=1), np.concatenate([-sin, cos], axis=1)], axis=0
            )
        )
    )
    kappa = np.arange(TOTAL).reshape(FACETS, WIDTH, 1) * np.ones((1, 1, 128))
    angle = np.pi * kappa / TOTAL
    rows = np.stack([np.cos(angle), np.sin(angle)], axis=1).astype(np.float32)
    q = float(FACETS * WIDTH * WIDTH) ** (-0.25)
    k = np.arange(WIDTH)
    numer = np.exp(2j * np.pi * (k % 3) / 3) - 1
    a = np.where(k % 3 == 0, 0, -0.5 * q * numer)
    b = np.where(k % 3 == 0, SUBGRID * q, -0.5j * q * numer)
    return twiddle, forward, backward, rows, a, b


def row_coefficients(a, b):
    return np.stack(
        [np.broadcast_to(v[:, None], (WIDTH, 128)) for v in (a.real, a.imag, b.real, b.imag)]
    ).astype(np.float32)


def image_rows(a, b):
    out = np.zeros((COLS, COLS, 2 * WIDTH, 128), ml_dtypes.bfloat16)
    k = np.arange(WIDTH)
    for mine in range(COLS):
        r = WIDTH * mine + np.arange(WIDTH)
        for c in range(COLS):
            phase = np.exp(2j * np.pi * ((r[:, None] * (k + WIDTH * c)[None, :]) % ROWS) / ROWS)
            phase = phase / math.sqrt(ROWS)
            full = np.zeros((WIDTH, 64), complex)
            full[:, :WIDTH] = phase * np.conj(b)[None, :]
            full[:, WIDTH] = phase @ np.conj(a)
            hi, lo = split_np(np.concatenate([full.real, full.imag], axis=0))
            out[mine, c, :, :64] = hi
            out[mine, c, :, 64:] = lo
    return out


def return_coefficients(b):
    lanes = np.arange(128)[None, :]
    sign = np.where(lanes < 64, 1.0, -1.0)
    br = np.broadcast_to(b.real[:, None], (WIDTH, 128))
    bi = b.imag[:, None] * sign
    live = (np.arange(WIDTH) % 3 != 0)[:, None]
    turn = np.where(live, -sign, 0.0)
    return np.stack([br, bi, turn]).astype(np.float32)


def half_turn(cell):
    z = (cell - 128.0) * (math.pi / 256)
    w = z * z
    s = 1.0 / math.factorial(13)
    for n in (11, 9, 7, 5, 3, 1):
        s = s * w + (1.0 if n % 4 == 1 else -1.0) / math.factorial(n)
    c = 1.0 / math.factorial(12)
    for n in (10, 8, 6, 4, 2, 0):
        c = c * w + (1.0 if n % 4 == 0 else -1.0) / math.factorial(n)
    return -(s * z), c


def cotangent(cx, sx, cy, sy, kappa, cell3, threes):
    ratio = (cx * cy + sx * sy) / (sx * cy - cx * sy)
    return jnp.where(threes, jnp.where(kappa == cell3, 1.0, 0.0), ratio)


def extract_kernel(col_ref, offset_ref, x_ref, tw_ref, f_ref, out_ref, mid, spectrum):
    mid[:, WIDTH:64, :] = jnp.zeros((16, 64 - WIDTH, 256), F32)
    for r in range(0, WIDTH, 8):
        xs = [
            (x_ref[0, r : r + 8, 128 * t : 128 * t + 128], x_ref[1, r : r + 8, 128 * t : 128 * t + 128])
            for t in range(16)
        ]
        ys = fft_list(xs, -1.0)
        for beta in range(16):
            yr, yi = ys[beta]
            c = tw_ref[0, beta : beta + 1, :]
            s = tw_ref[1, beta : beta + 1, :]
            mid[beta, r : r + 8, 0:128] = yr * c + yi * s
            mid[beta, r : r + 8, 128:256] = yi * c - yr * s
    left = (f_ref[0], f_ref[1])
    for beta in range(0, 16, 2):
        his, los = [], []
        for b in (beta, beta + 1):
            rh, rl = split(mid[b, :, 0:128])
            ih, il = split(mid[b, :, 128:256])
            his += [jnp.concatenate([rh, ih], axis=1), jnp.concatenate([ih, -rh], axis=1)]
            los += [jnp.concatenate([rl, il], axis=1), jnp.concatenate([il, -rl], axis=1)]
        right = (jnp.concatenate(his, axis=0), jnp.concatenate(los, axis=0))
        freq = dot3(left, right, transposed=True)
        spectrum[pl.ds(beta, 128, stride=16), :] = freq[:, 0:128]
        spectrum[pl.ds(beta + 1, 128, stride=16), :] = freq[:, 128:256]
    spectrum[LENGTH:PADDED, :] = spectrum[0:WIDTH, :]
    column = col_ref[1]
    for s in range(FACETS):
        out_ref[s] = spectrum[pl.ds(offset_ref[column, s], WIDTH), :]


def predict_kernel(k_ref, uv_ref, m_ref, rows_ref, coef_ref, res_ref, send_ref):
    uv = uv_ref[...].astype(F32)
    cy, sy = half_turn(uv)
    iota = lax.broadcasted_iota(jnp.int32, (WIDTH, 128), 0)
    threes = iota % 3 == 0
    kap = iota.astype(F32)
    ar, ai, br, bi = (coef_ref[n] for n in range(4))
    zeros = jnp.zeros((16, 128), F32)

    def one(f, acc):
        cx, sx = rows_ref[f, 0], rows_ref[f, 1]
        base = (f * WIDTH).astype(F32)
        pr, pi = [], []
        for n in range(2):
            cot = cotangent(
                cx, sx, cy[n : n + 1], sy[n : n + 1], kap + base, 3.0 * uv[n : n + 1], threes
            )
            pr.append(ar + br * cot)
            pi.append(ai + bi * cot)
        left = jnp.concatenate([pr[0], zeros, -pi[0], zeros], axis=0)
        right = jnp.concatenate([pi[0], zeros, pr[0], zeros], axis=0)
        mixed = split(jnp.concatenate([left, right], axis=1))
        t = dot3(split(k_ref[f]), mixed)
        tr, ti = t[:, :128], t[:, 128:]
        return (acc[0] + (tr * pr[1] - ti * pi[1]), acc[1] + (tr * pi[1] + ti * pr[1]))

    zero = jnp.zeros((WIDTH, 128), F32)
    sr, si = lax.fori_loop(0, FACETS, one, (zero, zero), unroll=4)
    res = jnp.concatenate(
        [
            m_ref[0:1] - jnp.sum(sr, axis=0, keepdims=True) * (1.0 / SUBGRID),
            m_ref[1:2] - jnp.sum(si, axis=0, keepdims=True) * (1.0 / SUBGRID),
        ],
        axis=0,
    )
    res_ref[...] = res
    send_ref[...] = jnp.broadcast_to(
        jnp.concatenate([res, uv], axis=0)[None], (FACETS * COLS, 4, 128)
    )


def image_kernel(
    pos_ref, offset_ref, got_ref, rows_ref, gamma_ref, coef_ref, tw_ref, b_ref, out_ref, grid, mid, trig
):
    grid[...] = jnp.zeros((PADDED, 128), F32)
    for n in range(2):
        cy, sy = half_turn(got_ref[:, 2 + n, :])
        trig[:, 2 * n, :] = cy
        trig[:, 2 * n + 1, :] = sy
    iota = lax.broadcasted_iota(jnp.int32, (WIDTH, 128), 0)
    threes = iota % 3 == 0
    kap = (iota + WIDTH * pos_ref[0]).astype(F32)
    cx, sx = rows_ref[0, 0], rows_ref[0, 1]
    one = jnp.where(lax.broadcasted_iota(jnp.int32, (16, 128), 0) == 0, 1.0, 0.0)
    one_h = one.astype(BF16)
    zero_h = jnp.zeros((16, 128), BF16)
    block_h = jnp.zeros((64, 128), BF16)
    br, bi, turn = coef_ref[0], coef_ref[1], coef_ref[2]
    group = 4

    def step(g, carry):
        for n in range(group):
            i = g * group + n
            c = i // FACETS
            s = i % FACETS
            got = got_ref[i]
            tr = trig[i]
            rr, ri, u, v = (got[m : m + 1] for m in range(4))
            cu = cotangent(cx, sx, tr[0:1], tr[1:2], kap, 3.0 * u, threes)
            cv = cotangent(cx, sx, tr[2:3], tr[3:4], kap, 3.0 * v, threes)
            uh, ul = split(cu)
            uh = jnp.concatenate([uh, one_h], axis=0)
            ul = jnp.concatenate([ul, zero_h], axis=0)
            right = jnp.concatenate(
                [jnp.concatenate([uh, ul], axis=1), jnp.concatenate([uh, block_h], axis=1)], axis=0
            )
            rowsum = dot(gamma_ref[0, c], right)
            rowsum = rowsum[:, :128] + rowsum[:, 128:]
            gr, gi = rowsum[:WIDTH], rowsum[WIDTH:]
            pad = jnp.zeros((64 - WIDTH, 128), F32)
            w = jnp.concatenate([gr * rr - gi * ri, pad, gr * ri + gi * rr, pad], axis=0)
            wh, wl = split(w)
            vh, vl = split(cv)
            vh = jnp.concatenate([vh, one_h], axis=0)
            left = jnp.concatenate(
                [jnp.concatenate([vh, vh], axis=1), jnp.concatenate([vl, jnp.zeros((WIDTH, 128), BF16)], axis=1)],
                axis=0,
            )
            h = dot(left, jnp.concatenate([wh, wl], axis=1), transposed=True)
            total = h[WIDTH : WIDTH + 1]
            h = h[:WIDTH] + h[64 : 64 + WIDTH] + turn * pltpu.roll(total, 64, 1)
            h = br * h + bi * pltpu.roll(h, 64, 1)
            o = offset_ref[c, s]
            grid[pl.ds(o, WIDTH), :] = grid[pl.ds(o, WIDTH), :] + h
        return carry

    lax.fori_loop(0, FACETS * COLS // group, step, 0)
    grid[0:WIDTH, :] = grid[0:WIDTH, :] + grid[LENGTH:PADDED, :]
    right = (b_ref[0], b_ref[1])
    for beta in range(16):
        d = grid[pl.ds(beta, 128, stride=16), :].T
        left = split(jnp.concatenate([d[0:WIDTH], d[64 : 64 + WIDTH]], axis=1))
        t = dot3(left, right)
        yr, yi = t[:, :128], t[:, 128:]
        c = tw_ref[0, beta : beta + 1, :]
        s = tw_ref[1, beta : beta + 1, :]
        mid[beta, :, 0:128] = yr * c - yi * s
        mid[beta, :, 128:256] = yi * c + yr * s
    for r in range(0, WIDTH, 8):
        ys = fft_list(
            [(mid[b, r : r + 8, 0:128], mid[b, r : r + 8, 128:256]) for b in range(16)], 1.0
        )
        for t in range(16):
            out_ref[0, r : r + 8, 128 * t : 128 * t + 128] = ys[t][0]
            out_ref[1, r : r + 8, 128 * t : 128 * t + 128] = ys[t][1]


def params():
    return pltpu.CompilerParams(vmem_limit_bytes=48 << 20)


VM = pltpu.MemorySpace.VMEM
SM = pltpu.MemorySpace.SMEM


def solution(mesh):
    twiddle, forward, backward, rows, a, b = tables()
    coef = row_coefficients(a, b)
    gamma = image_rows(a, b)
    ret = return_coefficients(b)

    def body(strips, sub_offset, uv_cells, measured):
        facet = lax.axis_index("facet")
        column = lax.axis_index("col")
        pos = jnp.stack([facet, column]).astype(jnp.int32)
        vm = pl.BlockSpec(memory_space=VM)
        sm = pl.BlockSpec(memory_space=SM)
        windows = pl.pallas_call(
            extract_kernel,
            out_shape=jax.ShapeDtypeStruct((FACETS, WIDTH, 128), F32),
            in_specs=[sm, sm, vm, vm, vm],
            out_specs=vm,
            scratch_shapes=[pltpu.VMEM((16, 64, 256), F32), pltpu.VMEM((PADDED, 128), F32)],
            compiler_params=params(),
            name="extract",
        )(pos, sub_offset, strips[0], jnp.asarray(twiddle), jnp.asarray(forward))
        arrived = lax.all_to_all(windows, "facet", split_axis=0, concat_axis=0, tiled=True)
        res, send = pl.pallas_call(
            predict_kernel,
            out_shape=(
                jax.ShapeDtypeStruct((2, 128), F32),
                jax.ShapeDtypeStruct((FACETS * COLS, 4, 128), F32),
            ),
            in_specs=[vm] * 5,
            out_specs=(vm, vm),
            compiler_params=params(),
            name="predict",
        )(arrived, uv_cells[0, 0], measured[0, 0], jnp.asarray(rows), jnp.asarray(coef))
        got = lax.all_to_all(send, ("col", "facet"), split_axis=0, concat_axis=0, tiled=True)
        image = pl.pallas_call(
            image_kernel,
            grid_spec=pltpu.PrefetchScalarGridSpec(
                num_scalar_prefetch=2,
                grid=(1,),
                in_specs=[
                    pl.BlockSpec((FACETS * COLS, 4, 128), lambda i, p, o: (0, 0, 0)),
                    pl.BlockSpec((1, 2, WIDTH, 128), lambda i, p, o: (p[0], 0, 0, 0)),
                    pl.BlockSpec((1, COLS, 2 * WIDTH, 128), lambda i, p, o: (p[1], 0, 0, 0)),
                    pl.BlockSpec((3, WIDTH, 128), lambda i, p, o: (0, 0, 0)),
                    pl.BlockSpec((2, 16, 128), lambda i, p, o: (0, 0, 0)),
                    pl.BlockSpec((2, 256, 256), lambda i, p, o: (0, 0, 0)),
                ],
                out_specs=pl.BlockSpec((2, WIDTH, LENGTH), lambda i, p, o: (0, 0, 0)),
                scratch_shapes=[
                    pltpu.VMEM((PADDED, 128), F32),
                    pltpu.VMEM((16, WIDTH, 256), F32),
                    pltpu.VMEM((FACETS * COLS, 4, 128), F32),
                ],
            ),
            out_shape=jax.ShapeDtypeStruct((2, WIDTH, LENGTH), F32),
            compiler_params=params(),
            name="image",
        )(
            pos,
            sub_offset,
            got,
            jnp.asarray(rows),
            jnp.asarray(gamma),
            jnp.asarray(ret),
            jnp.asarray(twiddle),
            jnp.asarray(backward),
        )
        return image[None], res[None, None]

    return jax.shard_map(
        body,
        mesh=mesh,
        in_specs=(
            P("facet", None, "col", None),
            P(),
            P("col", "facet", None, None),
            P("col", "facet", None, None),
        ),
        out_specs=(P("facet", None, "col", None), P("col", "facet", None, None)),
        check_vma=False,
    )
```

```python
import math

import jax
import jax.numpy as jnp
import ml_dtypes
import numpy as np
from jax import lax
from jax.experimental import pallas as pl
from jax.experimental.pallas import tpu as pltpu
from jax.sharding import PartitionSpec as P

SUBGRID = 256
WIDTH = 48
LENGTH = 2048
FACETS = 16
COLS = 8
GROUP = 16
ROWS = 384
PADDED = LENGTH + WIDTH
TOTAL = FACETS * WIDTH
F32 = jnp.float32
BF16 = jnp.bfloat16
ORDER = np.concatenate([np.arange(1, WIDTH, 3), np.arange(2, WIDTH, 3), np.arange(0, WIDTH, 3)])


def split_np(x):
    x = np.asarray(x, np.float32)
    hi = x.astype(ml_dtypes.bfloat16)
    lo = (x - hi.astype(np.float32)).astype(ml_dtypes.bfloat16)
    return hi, lo


def split(x):
    hi = x.astype(BF16)
    lo = (x - hi.astype(F32)).astype(BF16)
    return hi, lo


def dot(a, b, transposed=False):
    dims = (((1,), (1 if transposed else 0,)), ((), ()))
    return lax.dot_general(a, b, dims, preferred_element_type=F32)


def dot3(a, b, transposed=False):
    (ah, al), (bh, bl) = a, b
    return dot(ah, bh, transposed) + dot(ah, bl, transposed) + dot(al, bh, transposed)


def fft_list(xs, sign):
    n = len(xs)
    if n == 1:
        return xs
    even = fft_list(xs[0::2], sign)
    odd = fft_list(xs[1::2], sign)
    half = n // 2
    out = [None] * n
    for k in range(half):
        (er, ei), (r, i) = even[k], odd[k]
        if k == 0:
            tr, ti = r, i
        elif 4 * k == n:
            tr, ti = -sign * i, sign * r
        elif 8 * k == n:
            h = math.sqrt(0.5)
            tr, ti = h * (r - sign * i), h * (i + sign * r)
        elif 8 * k == 3 * n:
            h = math.sqrt(0.5)
            tr, ti = -h * (r + sign * i), h * (sign * r - i)
        else:
            c = math.cos(2 * math.pi * k / n)
            s = sign * math.sin(2 * math.pi * k / n)
            tr, ti = c * r - s * i, s * r + c * i
        out[k] = (er + tr, ei + ti)
        out[k + half] = (er - tr, ei - ti)
    return out


def tables():
    lane = np.arange(128)
    beta = np.arange(16)[:, None]
    ang = 2 * np.pi * ((lane[None, :] * beta) % LENGTH) / LENGTH
    norm = 1 / math.sqrt(LENGTH)
    twiddle = (np.stack([np.cos(ang), np.sin(ang)]) * norm).astype(np.float32)
    ang = 2 * np.pi * ((lane[:, None] * lane[None, :]) % 128) / 128
    cos, sin = np.cos(ang), np.sin(ang)
    forward = np.stack(split_np(np.concatenate([cos, sin], axis=1)))
    backward = np.stack(
        split_np(
            np.concatenate(
                [np.concatenate([cos, sin], axis=1), np.concatenate([-sin, cos], axis=1)], axis=0
            )
        )
    )
    kappa = np.arange(TOTAL).reshape(FACETS, WIDTH, 1) * np.ones((1, 1, 128))
    angle = np.pi * kappa / TOTAL
    rows = np.stack([np.cos(angle), np.sin(angle)], axis=1).astype(np.float32)
    live = np.ascontiguousarray(rows[:, :, ORDER[:32]])
    q = float(FACETS * WIDTH * WIDTH) ** (-0.25)
    k = np.arange(WIDTH)
    numer = np.exp(2j * np.pi * (k % 3) / 3) - 1
    a = np.where(k % 3 == 0, 0, -0.5 * q * numer)
    b = np.where(k % 3 == 0, SUBGRID * q, -0.5j * q * numer)
    return twiddle, forward, backward, rows, live, a, b


def row_coefficients(a, b):
    return np.stack(
        [np.broadcast_to(v[:, None], (WIDTH, 128)) for v in (a.real, a.imag, b.real, b.imag)]
    ).astype(np.float32)


def image_rows(a, b):
    out = np.zeros((COLS, COLS, 2 * WIDTH, 128), ml_dtypes.bfloat16)
    k = np.arange(WIDTH)
    for mine in range(COLS):
        r = WIDTH * mine + np.arange(WIDTH)
        for c in range(COLS):
            phase = np.exp(2j * np.pi * ((r[:, None] * (k + WIDTH * c)[None, :]) % ROWS) / ROWS)
            phase = phase / math.sqrt(ROWS)
            full = np.zeros((WIDTH, 64), complex)
            full[:, :WIDTH] = (phase * np.conj(b)[None, :])[:, ORDER]
            full[:, WIDTH] = phase @ np.conj(a)
            hi, lo = split_np(np.concatenate([full.real, full.imag], axis=0))
            out[mine, c, :, :64] = hi
            out[mine, c, :, 64:] = lo
    return out


def half_turn(cell):
    z = (cell - 128.0) * (math.pi / 256)
    w = z * z
    s = 1.0 / math.factorial(13)
    for n in (11, 9, 7, 5, 3, 1):
        s = s * w + (1.0 if n % 4 == 1 else -1.0) / math.factorial(n)
    c = 1.0 / math.factorial(12)
    for n in (10, 8, 6, 4, 2, 0):
        c = c * w + (1.0 if n % 4 == 0 else -1.0) / math.factorial(n)
    return -(s * z), c


def ratio(cx, sx, cy, sy):
    return (cx * cy + sx * sy) / (sx * cy - cx * sy)


def cotangent(cx, sx, cy, sy, kappa, cell3, threes):
    return jnp.where(threes, jnp.where(kappa == cell3, 1.0, 0.0), ratio(cx, sx, cy, sy))


def extract_kernel(
    col_ref, offset_hbm, x_hbm, tw_hbm, f_hbm, out_ref, mid, spectrum, offset_ref, x_ref, tw_ref, f_ref, sem
):
    copies = [pltpu.make_async_copy(tw_hbm, tw_ref, sem.at[6])]
    for n in range(6):
        rows = pl.ds(8 * n, 8)
        copies.append(pltpu.make_async_copy(x_hbm.at[:, rows, :], x_ref.at[:, rows, :], sem.at[n]))
    copies.append(pltpu.make_async_copy(f_hbm, f_ref, sem.at[7]))
    copies.append(pltpu.make_async_copy(offset_hbm, offset_ref, sem.at[8]))
    for copy in copies:
        copy.start()
    mid[:, WIDTH:64, :] = jnp.zeros((16, 64 - WIDTH, 256), F32)
    copies[0].wait()
    for r in range(0, WIDTH, 8):
        copies[1 + r // 8].wait()
        xs = [
            (x_ref[0, r : r + 8, 128 * t : 128 * t + 128], x_ref[1, r : r + 8, 128 * t : 128 * t + 128])
            for t in range(16)
        ]
        ys = fft_list(xs, -1.0)
        for beta in range(16):
            yr, yi = ys[beta]
            c = tw_ref[0, beta : beta + 1, :]
            s = tw_ref[1, beta : beta + 1, :]
            mid[beta, r : r + 8, 0:128] = yr * c + yi * s
            mid[beta, r : r + 8, 128:256] = yi * c - yr * s
    copies[7].wait()
    copies[8].wait()
    left = (f_ref[0], f_ref[1])
    for beta in range(0, 16, 2):
        his, los = [], []
        for b in (beta, beta + 1):
            rh, rl = split(mid[b, :, 0:128])
            ih, il = split(mid[b, :, 128:256])
            his += [jnp.concatenate([rh, ih], axis=1), jnp.concatenate([ih, -rh], axis=1)]
            los += [jnp.concatenate([rl, il], axis=1), jnp.concatenate([il, -rl], axis=1)]
        right = (jnp.concatenate(his, axis=0), jnp.concatenate(los, axis=0))
        freq = dot3(left, right, transposed=True)
        spectrum[pl.ds(beta, 128, stride=16), :] = freq[:, 0:128]
        spectrum[pl.ds(beta + 1, 128, stride=16), :] = freq[:, 128:256]
    spectrum[LENGTH:PADDED, :] = spectrum[0:WIDTH, :]
    column = col_ref[1]
    for s in range(FACETS):
        out_ref[s] = spectrum[pl.ds(offset_ref[column, s], WIDTH), :]


def predict_kernel(k_ref, uv_ref, m_ref, rows_ref, coef_ref, res_ref, send_ref):
    uv = uv_ref[...].astype(F32)
    cy, sy = half_turn(uv)
    iota = lax.broadcasted_iota(jnp.int32, (WIDTH, 128), 0)
    threes = iota % 3 == 0
    kap = iota.astype(F32)
    ar, ai, br, bi = (coef_ref[n] for n in range(4))
    zeros = jnp.zeros((16, 128), F32)

    def one(f, acc):
        cx, sx = rows_ref[f, 0], rows_ref[f, 1]
        base = (f * WIDTH).astype(F32)
        pr, pi = [], []
        for n in range(2):
            cot = cotangent(
                cx, sx, cy[n : n + 1], sy[n : n + 1], kap + base, 3.0 * uv[n : n + 1], threes
            )
            pr.append(ar + br * cot)
            pi.append(ai + bi * cot)
        left = jnp.concatenate([pr[0], zeros, -pi[0], zeros], axis=0)
        right = jnp.concatenate([pi[0], zeros, pr[0], zeros], axis=0)
        mixed = split(jnp.concatenate([left, right], axis=1))
        t = dot3(split(k_ref[f]), mixed)
        tr, ti = t[:, :128], t[:, 128:]
        return (acc[0] + (tr * pr[1] - ti * pi[1]), acc[1] + (tr * pi[1] + ti * pr[1]))

    zero = jnp.zeros((WIDTH, 128), F32)
    sr, si = lax.fori_loop(0, FACETS, one, (zero, zero), unroll=4)
    res = jnp.concatenate(
        [
            m_ref[0:1] - jnp.sum(sr, axis=0, keepdims=True) * (1.0 / SUBGRID),
            m_ref[1:2] - jnp.sum(si, axis=0, keepdims=True) * (1.0 / SUBGRID),
        ],
        axis=0,
    )
    res_ref[...] = res
    send_ref[...] = jnp.broadcast_to(
        jnp.concatenate([res, uv], axis=0)[None], (FACETS * COLS, 4, 128)
    )


def image_kernel(
    pos_ref, offset_ref, got_ref, live_ref, gamma_ref, tw_ref, b_ref, out_ref, grid, mid, trig
):
    grid[...] = jnp.zeros((3, PADDED, 128), F32)
    for n in range(2):
        cy, sy = half_turn(got_ref[:, 2 + n, :])
        trig[:, 2 * n, :] = cy
        trig[:, 2 * n + 1, :] = sy
    iota = lax.broadcasted_iota(jnp.int32, (16, 128), 0)
    kap = (iota + 16 * pos_ref[0]).astype(F32)
    cx, sx = live_ref[0, 0], live_ref[0, 1]
    one_h = jnp.where(iota == 0, 1.0, 0.0).astype(BF16)
    none_h = jnp.zeros((32, 128), BF16)
    pad = jnp.zeros((64 - WIDTH, 128), F32)
    lanes = lax.broadcasted_iota(jnp.int32, (1, 128), 1)
    turn = jnp.where(lanes < 64, -1.0, 1.0)

    def parts(cy, sy, cell):
        hi, lo = split(ratio(cx, sx, cy, sy))
        hit = jnp.where(kap == cell, 1.0, 0.0).astype(BF16)
        return jnp.concatenate([hi, hit, one_h], axis=0), lo

    def step(g, carry):
        c = (g * GROUP) // FACETS
        s = (g * GROUP) % FACETS
        gam = gamma_ref[0, c]
        gam = jnp.concatenate([gam, gam[:, :32]], axis=1)
        gots = [got_ref[g * GROUP + n] for n in range(GROUP)]
        trigs = [trig[g * GROUP + n] for n in range(GROUP)]
        us = [parts(t[0:1], t[1:2], r[2:3]) for r, t in zip(gots, trigs)]
        gs = [dot(gam, jnp.concatenate([h, h, l], axis=0)) for h, l in us]
        vs = [parts(t[2:3], t[3:4], r[3:4]) for r, t in zip(gots, trigs)]
        hs = []
        for n in range(GROUP):
            rr, ri = gots[n][0:1], gots[n][1:2]
            gr, gi = gs[n][:WIDTH], gs[n][WIDTH:]
            w = jnp.concatenate([gr * rr - gi * ri, pad, gr * ri + gi * rr, pad], axis=0)
            wh, wl = split(w)
            vh, vl = vs[n]
            left = jnp.concatenate(
                [jnp.concatenate([vh, vh], axis=1), jnp.concatenate([vl, none_h], axis=1)], axis=0
            )
            hs.append(dot(left, jnp.concatenate([wh, wl], axis=1), transposed=True))
        for n in range(GROUP):
            h = hs[n]
            total = turn * pltpu.roll(h[WIDTH : WIDTH + 1], 64, 1)
            o = offset_ref[c, s + n]
            for m in range(3):
                add = h[16 * m : 16 * m + 16]
                if m < 2:
                    add = add + h[64 + 16 * m : 80 + 16 * m] + total
                at = pl.ds(o + (m + 1) % 3, 16, stride=3)
                grid[m, at, :] = grid[m, at, :] + add
        return carry

    lax.fori_loop(0, FACETS * COLS // GROUP, step, 0)
    grid[:, 0:WIDTH, :] = grid[:, 0:WIDTH, :] + grid[:, LENGTH:PADDED, :]
    q = float(FACETS * WIDTH * WIDTH) ** (-0.25)
    right = (b_ref[0], b_ref[1])
    for beta in range(16):
        one, two, nil = (grid[m, pl.ds(beta, 128, stride=16), :] for m in range(3))
        d = (SUBGRID * q) * nil + (q * math.sqrt(3) / 4) * (one - two)
        d = (d - (0.75 * q) * turn * pltpu.roll(one + two, 64, 1)).T
        left = split(jnp.concatenate([d[0:WIDTH], d[64 : 64 + WIDTH]], axis=1))
        t = dot3(left, right)
        yr, yi = t[:, :128], t[:, 128:]
        c = tw_ref[0, beta : beta + 1, :]
        s = tw_ref[1, beta : beta + 1, :]
        mid[beta, :, 0:128] = yr * c - yi * s
        mid[beta, :, 128:256] = yi * c + yr * s
    for r in range(0, WIDTH, 8):
        ys = fft_list(
            [(mid[b, r : r + 8, 0:128], mid[b, r : r + 8, 128:256]) for b in range(16)], 1.0
        )
        for t in range(16):
            out_ref[0, r : r + 8, 128 * t : 128 * t + 128] = ys[t][0]
            out_ref[1, r : r + 8, 128 * t : 128 * t + 128] = ys[t][1]


def keep(x):
    return pltpu.with_memory_space_constraint(x, pltpu.MemorySpace.HBM)


def params():
    return pltpu.CompilerParams(vmem_limit_bytes=48 << 20)


VM = pltpu.MemorySpace.VMEM
SM = pltpu.MemorySpace.SMEM


def solution(mesh):
    twiddle, forward, backward, rows, live, a, b = tables()
    coef = row_coefficients(a, b)
    gamma = image_rows(a, b)

    def body(strips, sub_offset, uv_cells, measured):
        facet = lax.axis_index("facet")
        column = lax.axis_index("col")
        pos = jnp.stack([facet, column]).astype(jnp.int32)
        vm = pl.BlockSpec(memory_space=VM)
        sm = pl.BlockSpec(memory_space=SM)
        hbm = pl.BlockSpec(memory_space=pltpu.MemorySpace.HBM)
        windows = pl.pallas_call(
            extract_kernel,
            out_shape=jax.ShapeDtypeStruct((FACETS, WIDTH, 128), F32),
            in_specs=[sm, hbm, hbm, hbm, hbm],
            out_specs=vm,
            scratch_shapes=[
                pltpu.VMEM((16, 64, 256), F32),
                pltpu.VMEM((PADDED, 128), F32),
                pltpu.SMEM((COLS, FACETS), jnp.int32),
                pltpu.VMEM((2, WIDTH, LENGTH), F32),
                pltpu.VMEM((2, 16, 128), F32),
                pltpu.VMEM((2, 128, 256), BF16),
                pltpu.SemaphoreType.DMA((9,)),
            ],
            compiler_params=params(),
            name="extract",
        )(pos, *(keep(x) for x in (sub_offset, strips[0], jnp.asarray(twiddle), jnp.asarray(forward))))
        arrived = lax.all_to_all(windows, "facet", split_axis=0, concat_axis=0, tiled=True)
        res, send = pl.pallas_call(
            predict_kernel,
            out_shape=(
                jax.ShapeDtypeStruct((2, 128), F32),
                jax.ShapeDtypeStruct((FACETS * COLS, 4, 128), F32),
            ),
            in_specs=[vm] * 5,
            out_specs=(vm, vm),
            compiler_params=params(),
            name="predict",
        )(arrived, uv_cells[0, 0], measured[0, 0], jnp.asarray(rows), jnp.asarray(coef))
        got = lax.all_to_all(send, ("col", "facet"), split_axis=0, concat_axis=0, tiled=True)
        image = pl.pallas_call(
            image_kernel,
            grid_spec=pltpu.PrefetchScalarGridSpec(
                num_scalar_prefetch=2,
                grid=(1,),
                in_specs=[
                    pl.BlockSpec((FACETS * COLS, 4, 128), lambda i, p, o: (0, 0, 0)),
                    pl.BlockSpec((1, 2, 32, 128), lambda i, p, o: (p[0], 0, 0, 0)),
                    pl.BlockSpec((1, COLS, 2 * WIDTH, 128), lambda i, p, o: (p[1], 0, 0, 0)),
                    pl.BlockSpec((2, 16, 128), lambda i, p, o: (0, 0, 0)),
                    pl.BlockSpec((2, 256, 256), lambda i, p, o: (0, 0, 0)),
                ],
                out_specs=pl.BlockSpec((2, WIDTH, LENGTH), lambda i, p, o: (0, 0, 0)),
                scratch_shapes=[
                    pltpu.VMEM((3, PADDED, 128), F32),
                    pltpu.VMEM((16, WIDTH, 256), F32),
                    pltpu.VMEM((FACETS * COLS, 4, 128), F32),
                ],
            ),
            out_shape=jax.ShapeDtypeStruct((2, WIDTH, LENGTH), F32),
            compiler_params=params(),
            name="image",
        )(
            pos,
            sub_offset,
            got,
            jnp.asarray(live),
            jnp.asarray(gamma),
            jnp.asarray(twiddle),
            jnp.asarray(backward),
        )
        return image[None], res[None, None]

    return jax.shard_map(
        body,
        mesh=mesh,
        in_specs=(
            P("facet", None, "col", None),
            P(),
            P("col", "facet", None, None),
            P("col", "facet", None, None),
        ),
        out_specs=(P("facet", None, "col", None), P("col", "facet", None, None)),
        check_vma=False,
    )
```

```python
import math

import jax
import jax.numpy as jnp
import ml_dtypes
import numpy as np
from jax import lax
from jax.experimental import pallas as pl
from jax.experimental.pallas import tpu as pltpu
from jax.sharding import PartitionSpec as P

SUBGRID = 256
WIDTH = 48
LENGTH = 2048
FACETS = 16
COLS = 8
GROUP = 32
ROWS = 384
PADDED = LENGTH + WIDTH
TOTAL = FACETS * WIDTH
F32 = jnp.float32
BF16 = jnp.bfloat16
ORDER = np.concatenate([np.arange(1, WIDTH, 3), np.arange(2, WIDTH, 3), np.arange(0, WIDTH, 3)])


def split_np(x):
    x = np.asarray(x, np.float32)
    hi = x.astype(ml_dtypes.bfloat16)
    lo = (x - hi.astype(np.float32)).astype(ml_dtypes.bfloat16)
    return hi, lo


def split(x):
    hi = x.astype(BF16)
    lo = (x - hi.astype(F32)).astype(BF16)
    return hi, lo


def dot(a, b, transposed=False):
    dims = (((1,), (1 if transposed else 0,)), ((), ()))
    return lax.dot_general(a, b, dims, preferred_element_type=F32)


def dot3(a, b, transposed=False):
    (ah, al), (bh, bl) = a, b
    return dot(ah, bh, transposed) + dot(ah, bl, transposed) + dot(al, bh, transposed)


def fft_list(xs, sign):
    n = len(xs)
    if n == 1:
        return xs
    even = fft_list(xs[0::2], sign)
    odd = fft_list(xs[1::2], sign)
    half = n // 2
    out = [None] * n
    for k in range(half):
        (er, ei), (r, i) = even[k], odd[k]
        if k == 0:
            tr, ti = r, i
        elif 4 * k == n:
            tr, ti = -sign * i, sign * r
        elif 8 * k == n:
            h = math.sqrt(0.5)
            tr, ti = h * (r - sign * i), h * (i + sign * r)
        elif 8 * k == 3 * n:
            h = math.sqrt(0.5)
            tr, ti = -h * (r + sign * i), h * (sign * r - i)
        else:
            c = math.cos(2 * math.pi * k / n)
            s = sign * math.sin(2 * math.pi * k / n)
            tr, ti = c * r - s * i, s * r + c * i
        out[k] = (er + tr, ei + ti)
        out[k + half] = (er - tr, ei - ti)
    return out


def tables():
    lane = np.arange(128)
    beta = np.arange(16)[:, None]
    ang = 2 * np.pi * ((lane[None, :] * beta) % LENGTH) / LENGTH
    norm = 1 / math.sqrt(LENGTH)
    twiddle = (np.stack([np.cos(ang), np.sin(ang)]) * norm).astype(np.float32)
    ang = 2 * np.pi * ((lane[:, None] * lane[None, :]) % 128) / 128
    cos, sin = np.cos(ang), np.sin(ang)
    forward = np.stack(split_np(np.concatenate([cos, sin], axis=1)))
    backward = np.stack(
        split_np(
            np.concatenate(
                [np.concatenate([cos, sin], axis=1), np.concatenate([-sin, cos], axis=1)], axis=0
            )
        )
    )
    kappa = np.arange(TOTAL).reshape(FACETS, WIDTH, 1) * np.ones((1, 1, 128))
    angle = np.pi * kappa / TOTAL
    rows = np.stack([np.cos(angle), np.sin(angle)], axis=1).astype(np.float32)
    live = np.ascontiguousarray(rows[:, :, ORDER[:32]])
    q = float(FACETS * WIDTH * WIDTH) ** (-0.25)
    k = np.arange(WIDTH)
    numer = np.exp(2j * np.pi * (k % 3) / 3) - 1
    a = np.where(k % 3 == 0, 0, -0.5 * q * numer)
    b = np.where(k % 3 == 0, SUBGRID * q, -0.5j * q * numer)
    return twiddle, forward, backward, rows, live, a, b


def row_coefficients(a, b):
    return np.stack(
        [np.broadcast_to(v[:, None], (WIDTH, 128)) for v in (a.real, a.imag, b.real, b.imag)]
    ).astype(np.float32)


def image_rows(a, b):
    out = np.zeros((COLS, COLS, 2 * WIDTH, 128), ml_dtypes.bfloat16)
    k = np.arange(WIDTH)
    for mine in range(COLS):
        r = WIDTH * mine + np.arange(WIDTH)
        for c in range(COLS):
            phase = np.exp(2j * np.pi * ((r[:, None] * (k + WIDTH * c)[None, :]) % ROWS) / ROWS)
            phase = phase / math.sqrt(ROWS)
            full = np.zeros((WIDTH, 64), complex)
            full[:, :WIDTH] = (phase * np.conj(b)[None, :])[:, ORDER]
            full[:, WIDTH] = phase @ np.conj(a)
            hi, lo = split_np(np.concatenate([full.real, full.imag], axis=0))
            out[mine, c, :, :64] = hi
            out[mine, c, :, 64:] = lo
    return out


def half_turn(cell):
    z = (cell - 128.0) * (math.pi / 256)
    w = z * z
    s = 1.0 / math.factorial(13)
    for n in (11, 9, 7, 5, 3, 1):
        s = s * w + (1.0 if n % 4 == 1 else -1.0) / math.factorial(n)
    c = 1.0 / math.factorial(12)
    for n in (10, 8, 6, 4, 2, 0):
        c = c * w + (1.0 if n % 4 == 0 else -1.0) / math.factorial(n)
    return -(s * z), c


def ratio(cx, sx, cy, sy):
    return (cx * cy + sx * sy) / (sx * cy - cx * sy)


def cotangent(cx, sx, cy, sy, kappa, cell3, threes):
    return jnp.where(threes, jnp.where(kappa == cell3, 1.0, 0.0), ratio(cx, sx, cy, sy))


def extract_kernel(
    col_ref, offset_hbm, x_hbm, tw_hbm, f_hbm, out_ref, mid, spectrum, offset_ref, x_ref, tw_ref, f_ref, sem
):
    copies = [pltpu.make_async_copy(tw_hbm, tw_ref, sem.at[6])]
    for n in range(6):
        rows = pl.ds(8 * n, 8)
        copies.append(pltpu.make_async_copy(x_hbm.at[:, rows, :], x_ref.at[:, rows, :], sem.at[n]))
    copies.append(pltpu.make_async_copy(f_hbm, f_ref, sem.at[7]))
    copies.append(pltpu.make_async_copy(offset_hbm, offset_ref, sem.at[8]))
    for copy in copies:
        copy.start()
    mid[:, WIDTH:64, :] = jnp.zeros((16, 64 - WIDTH, 256), F32)
    copies[0].wait()
    for r in range(0, WIDTH, 8):
        copies[1 + r // 8].wait()
        xs = [
            (x_ref[0, r : r + 8, 128 * t : 128 * t + 128], x_ref[1, r : r + 8, 128 * t : 128 * t + 128])
            for t in range(16)
        ]
        ys = fft_list(xs, -1.0)
        for beta in range(16):
            yr, yi = ys[beta]
            c = tw_ref[0, beta : beta + 1, :]
            s = tw_ref[1, beta : beta + 1, :]
            mid[beta, r : r + 8, 0:128] = yr * c + yi * s
            mid[beta, r : r + 8, 128:256] = yi * c - yr * s
    copies[7].wait()
    copies[8].wait()
    left = (f_ref[0], f_ref[1])
    rights = []
    for beta in range(0, 16, 2):
        his, los = [], []
        for b in (beta, beta + 1):
            rh, rl = split(mid[b, :, 0:128])
            ih, il = split(mid[b, :, 128:256])
            his += [jnp.concatenate([rh, ih], axis=1), jnp.concatenate([ih, -rh], axis=1)]
            los += [jnp.concatenate([rl, il], axis=1), jnp.concatenate([il, -rl], axis=1)]
        rights.append((jnp.concatenate(his, axis=0), jnp.concatenate(los, axis=0)))
    freqs = [dot3(left, right, transposed=True) for right in rights]
    for beta in range(16):
        half = 128 * (beta % 2)
        spectrum[pl.ds(beta, 128, stride=16), :] = freqs[beta // 2][:, half : half + 128]
    spectrum[LENGTH:PADDED, :] = spectrum[0:WIDTH, :]
    column = col_ref[1]
    for s in range(FACETS):
        out_ref[s] = spectrum[pl.ds(offset_ref[column, s], WIDTH), :]


def predict_kernel(k_ref, uv_ref, m_ref, rows_ref, coef_ref, res_ref, send_ref):
    uv = uv_ref[...].astype(F32)
    cy, sy = half_turn(uv)
    iota = lax.broadcasted_iota(jnp.int32, (WIDTH, 128), 0)
    threes = iota % 3 == 0
    kap = iota.astype(F32)
    ar, ai, br, bi = (coef_ref[n] for n in range(4))
    zeros = jnp.zeros((16, 128), F32)

    mixes, others = [], []
    for f in range(FACETS):
        cx, sx = rows_ref[f, 0], rows_ref[f, 1]
        pr, pi = [], []
        for n in range(2):
            cell = 3.0 * uv[n : n + 1] - float(f * WIDTH)
            cot = cotangent(cx, sx, cy[n : n + 1], sy[n : n + 1], kap, cell, threes)
            pr.append(ar + br * cot)
            pi.append(ai + bi * cot)
        left = jnp.concatenate([pr[0], zeros, -pi[0], zeros], axis=0)
        right = jnp.concatenate([pi[0], zeros, pr[0], zeros], axis=0)
        mixes.append(split(jnp.concatenate([left, right], axis=1)))
        others.append((pr[1], pi[1]))
    sums = [dot3(split(k_ref[f]), mixes[f]) for f in range(FACETS)]
    sr = jnp.zeros((WIDTH, 128), F32)
    si = jnp.zeros((WIDTH, 128), F32)
    for f in range(FACETS):
        tr, ti = sums[f][:, :128], sums[f][:, 128:]
        pr, pi = others[f]
        sr = sr + (tr * pr - ti * pi)
        si = si + (tr * pi + ti * pr)
    res = jnp.concatenate(
        [
            m_ref[0:1] - jnp.sum(sr, axis=0, keepdims=True) * (1.0 / SUBGRID),
            m_ref[1:2] - jnp.sum(si, axis=0, keepdims=True) * (1.0 / SUBGRID),
        ],
        axis=0,
    )
    res_ref[...] = res
    send_ref[...] = jnp.broadcast_to(
        jnp.concatenate([res, uv], axis=0)[None], (FACETS * COLS, 4, 128)
    )


def image_kernel(
    pos_ref, offset_ref, got_ref, live_ref, gamma_ref, tw_ref, b_ref, out_hbm, grid, mid, out_ref, sem
):
    facet, column = pos_ref[0], pos_ref[1]
    grid[...] = jnp.zeros((3, PADDED, 128), F32)
    iota = lax.broadcasted_iota(jnp.int32, (16, 128), 0)
    kap = (iota + 16 * facet).astype(F32)
    cx, sx = live_ref[facet, 0], live_ref[facet, 1]
    one_h = jnp.where(iota == 0, 1.0, 0.0).astype(BF16)
    none_h = jnp.zeros((32, 128), BF16)
    pad = jnp.zeros((64 - WIDTH, 128), F32)
    lanes = lax.broadcasted_iota(jnp.int32, (1, 128), 1)
    turn = jnp.where(lanes < 64, -1.0, 1.0)

    def parts(cy, sy, cell):
        hi, lo = split(ratio(cx, sx, cy, sy))
        hit = jnp.where(kap == cell, 1.0, 0.0).astype(BF16)
        return jnp.concatenate([hi, hit, one_h], axis=0), lo

    def step(g, carry):
        first = g * (GROUP // FACETS)
        gots, turns = [], []
        for n in range(GROUP):
            got = got_ref[g * GROUP + n]
            cy, sy = half_turn(got)
            gots.append([got[r : r + 1] for r in range(4)])
            turns.append([(cy[r : r + 1], sy[r : r + 1]) for r in (2, 3)])
        gs, vs, hs = {}, {}, {}
        for b in range(0, GROUP, FACETS):
            gam = gamma_ref[column, first + b // FACETS]
            gam = jnp.concatenate([gam, gam[:, :32]], axis=1)
            for n in range(b, b + FACETS):
                h, l = parts(*turns[n][0], gots[n][2])
                gs[n] = dot(gam, jnp.concatenate([h, h, l], axis=0))
            for n in range(b, b + FACETS):
                vs[n] = parts(*turns[n][1], gots[n][3])
            for n in range(b, b + FACETS):
                rr, ri = gots[n][0], gots[n][1]
                gr, gi = gs[n][:WIDTH], gs[n][WIDTH:]
                w = jnp.concatenate([gr * rr - gi * ri, pad, gr * ri + gi * rr, pad], axis=0)
                wh, wl = split(w)
                vh, vl = vs[n]
                left = jnp.concatenate(
                    [jnp.concatenate([vh, vh], axis=1), jnp.concatenate([vl, none_h], axis=1)], axis=0
                )
                hs[n] = dot(left, jnp.concatenate([wh, wl], axis=1), transposed=True)
            for n in range(b, b + FACETS):
                h = hs[n]
                total = turn * pltpu.roll(h[WIDTH : WIDTH + 1], 64, 1)
                o = offset_ref[first + b // FACETS, n % FACETS]
                for m in range(3):
                    add = h[16 * m : 16 * m + 16]
                    if m < 2:
                        add = add + h[64 + 16 * m : 80 + 16 * m] + total
                    at = pl.ds(o + (m + 1) % 3, 16, stride=3)
                    grid[m, at, :] = grid[m, at, :] + add
        return carry

    lax.fori_loop(0, FACETS * COLS // GROUP, step, 0)
    grid[:, 0:WIDTH, :] = grid[:, 0:WIDTH, :] + grid[:, LENGTH:PADDED, :]
    q = float(FACETS * WIDTH * WIDTH) ** (-0.25)
    right = (b_ref[0], b_ref[1])
    lefts = []
    for beta in range(16):
        one, two, nil = (grid[m, pl.ds(beta, 128, stride=16), :] for m in range(3))
        d = (SUBGRID * q) * nil + (q * math.sqrt(3) / 4) * (one - two)
        d = (d - (0.75 * q) * turn * pltpu.roll(one + two, 64, 1)).T
        lefts.append(split(jnp.concatenate([d[0:WIDTH], d[64 : 64 + WIDTH]], axis=1)))
    freqs = [dot3(left, right) for left in lefts]
    for beta in range(16):
        yr, yi = freqs[beta][:, :128], freqs[beta][:, 128:]
        c = tw_ref[0, beta : beta + 1, :]
        s = tw_ref[1, beta : beta + 1, :]
        mid[beta, :, 0:128] = yr * c - yi * s
        mid[beta, :, 128:256] = yi * c + yr * s
    copies = []
    for r in range(0, WIDTH, 8):
        ys = fft_list(
            [(mid[b, r : r + 8, 0:128], mid[b, r : r + 8, 128:256]) for b in range(16)], 1.0
        )
        for t in range(16):
            out_ref[0, r : r + 8, 128 * t : 128 * t + 128] = ys[t][0]
            out_ref[1, r : r + 8, 128 * t : 128 * t + 128] = ys[t][1]
        rows = pl.ds(r, 8)
        copies.append(
            pltpu.make_async_copy(out_ref.at[:, rows, :], out_hbm.at[:, rows, :], sem.at[r // 8])
        )
        copies[-1].start()
    for copy in copies:
        copy.wait()


def keep(x):
    return pltpu.with_memory_space_constraint(x, pltpu.MemorySpace.HBM)


def params():
    return pltpu.CompilerParams(vmem_limit_bytes=48 << 20)


VM = pltpu.MemorySpace.VMEM
SM = pltpu.MemorySpace.SMEM


def solution(mesh):
    twiddle, forward, backward, rows, live, a, b = tables()
    coef = row_coefficients(a, b)
    gamma = image_rows(a, b)

    def body(strips, sub_offset, uv_cells, measured):
        pos = jnp.stack([lax.axis_index("facet"), lax.axis_index("col")]).astype(jnp.int32)
        vm = pl.BlockSpec(memory_space=VM)
        sm = pl.BlockSpec(memory_space=SM)
        hbm = pl.BlockSpec(memory_space=pltpu.MemorySpace.HBM)
        windows = pl.pallas_call(
            extract_kernel,
            out_shape=jax.ShapeDtypeStruct((FACETS, WIDTH, 128), F32),
            in_specs=[sm, hbm, hbm, hbm, hbm],
            out_specs=vm,
            scratch_shapes=[
                pltpu.VMEM((16, 64, 256), F32),
                pltpu.VMEM((PADDED, 128), F32),
                pltpu.SMEM((COLS, FACETS), jnp.int32),
                pltpu.VMEM((2, WIDTH, LENGTH), F32),
                pltpu.VMEM((2, 16, 128), F32),
                pltpu.VMEM((2, 128, 256), BF16),
                pltpu.SemaphoreType.DMA((9,)),
            ],
            compiler_params=params(),
            name="extract",
        )(pos, *(keep(x) for x in (sub_offset, strips[0], jnp.asarray(twiddle), jnp.asarray(forward))))
        arrived = lax.all_to_all(windows, "facet", split_axis=0, concat_axis=0, tiled=True)
        res, send = pl.pallas_call(
            predict_kernel,
            out_shape=(
                jax.ShapeDtypeStruct((2, 128), F32),
                jax.ShapeDtypeStruct((FACETS * COLS, 4, 128), F32),
            ),
            in_specs=[vm] * 5,
            out_specs=(vm, vm),
            compiler_params=params(),
            name="predict",
        )(arrived, uv_cells[0, 0], measured[0, 0], jnp.asarray(rows), jnp.asarray(coef))
        got = lax.all_to_all(send, ("col", "facet"), split_axis=0, concat_axis=0, tiled=True)
        image = pl.pallas_call(
            image_kernel,
            out_shape=jax.ShapeDtypeStruct((2, WIDTH, LENGTH), F32),
            in_specs=[sm, sm, vm, vm, vm, vm, vm],
            out_specs=pl.BlockSpec(memory_space=pl.ANY),
            scratch_shapes=[
                pltpu.VMEM((3, PADDED, 128), F32),
                pltpu.VMEM((16, WIDTH, 256), F32),
                pltpu.VMEM((2, WIDTH, LENGTH), F32),
                pltpu.SemaphoreType.DMA((6,)),
            ],
            compiler_params=params(),
            name="image",
        )(
            pos,
            sub_offset,
            got,
            jnp.asarray(live),
            jnp.asarray(gamma),
            jnp.asarray(twiddle),
            jnp.asarray(backward),
        )
        return image[None], res[None, None]

    return jax.shard_map(
        body,
        mesh=mesh,
        in_specs=(
            P("facet", None, "col", None),
            P(),
            P("col", "facet", None, None),
            P("col", "facet", None, None),
        ),
        out_specs=(P("facet", None, "col", None), P("col", "facet", None, None)),
        check_vma=False,
    )
```

```python
import math

import jax
import jax.numpy as jnp
import ml_dtypes
import numpy as np
from jax import lax
from jax.experimental import pallas as pl
from jax.experimental.pallas import tpu as pltpu
from jax.sharding import PartitionSpec as P

SUBGRID = 256
WIDTH = 48
LENGTH = 2048
FACETS = 16
COLS = 8
GROUP = 128
LAG1 = 8
LAG2 = 16
ROWS = 384
PADDED = LENGTH + WIDTH
TOTAL = FACETS * WIDTH
F32 = jnp.float32
BF16 = jnp.bfloat16
ORDER = np.concatenate([np.arange(1, WIDTH, 3), np.arange(2, WIDTH, 3), np.arange(0, WIDTH, 3)])


def split_np(x):
    x = np.asarray(x, np.float32)
    hi = x.astype(ml_dtypes.bfloat16)
    lo = (x - hi.astype(np.float32)).astype(ml_dtypes.bfloat16)
    return hi, lo


def split(x):
    hi = x.astype(BF16)
    lo = (x - hi.astype(F32)).astype(BF16)
    return hi, lo


def dot(a, b, transposed=False):
    dims = (((1,), (1 if transposed else 0,)), ((), ()))
    return lax.dot_general(a, b, dims, preferred_element_type=F32)


def dot3(a, b, transposed=False):
    (ah, al), (bh, bl) = a, b
    rows = ah.shape[0]
    both = dot(jnp.concatenate([ah, al], axis=0), bh, transposed)
    return both[:rows] + both[rows:] + dot(ah, bl, transposed)


def fft_list(xs, sign):
    n = len(xs)
    if n == 1:
        return xs
    even = fft_list(xs[0::2], sign)
    odd = fft_list(xs[1::2], sign)
    half = n // 2
    out = [None] * n
    for k in range(half):
        (er, ei), (r, i) = even[k], odd[k]
        if k == 0:
            tr, ti = r, i
        elif 4 * k == n:
            tr, ti = -sign * i, sign * r
        elif 8 * k == n:
            h = math.sqrt(0.5)
            tr, ti = h * (r - sign * i), h * (i + sign * r)
        elif 8 * k == 3 * n:
            h = math.sqrt(0.5)
            tr, ti = -h * (r + sign * i), h * (sign * r - i)
        else:
            c = math.cos(2 * math.pi * k / n)
            s = sign * math.sin(2 * math.pi * k / n)
            tr, ti = c * r - s * i, s * r + c * i
        out[k] = (er + tr, ei + ti)
        out[k + half] = (er - tr, ei - ti)
    return out


def tables():
    lane = np.arange(128)
    beta = np.arange(16)[:, None]
    ang = 2 * np.pi * ((lane[None, :] * beta) % LENGTH) / LENGTH
    norm = 1 / math.sqrt(LENGTH)
    twiddle = (np.stack([np.cos(ang), np.sin(ang)]) * norm).astype(np.float32)
    ang = 2 * np.pi * ((lane[:, None] * lane[None, :]) % 128) / 128
    cos, sin = np.cos(ang), np.sin(ang)
    forward = np.stack(split_np(np.concatenate([cos, sin], axis=1)))
    backward = np.stack(
        split_np(
            np.concatenate(
                [np.concatenate([cos, sin], axis=1), np.concatenate([-sin, cos], axis=1)], axis=0
            )
        )
    )
    kappa = np.arange(TOTAL).reshape(FACETS, WIDTH, 1) * np.ones((1, 1, 128))
    angle = np.pi * kappa / TOTAL
    cot = np.where(kappa % 3 == 0, 0.0, 1 / np.tan(np.where(kappa % 3 == 0, 1.0, angle)))
    rows = cot.astype(np.float32)
    live = np.ascontiguousarray(rows[:, ORDER[:32]])
    q = float(FACETS * WIDTH * WIDTH) ** (-0.25)
    k = np.arange(WIDTH)
    numer = np.exp(2j * np.pi * (k % 3) / 3) - 1
    a = np.where(k % 3 == 0, 0, -0.5 * q * numer)
    b = np.where(k % 3 == 0, SUBGRID * q, -0.5j * q * numer)
    return twiddle, forward, backward, rows, live, a, b


def row_coefficients(a, b):
    return np.stack(
        [np.broadcast_to(v[:, None], (WIDTH, 128)) for v in (a.real, a.imag, b.real, b.imag)]
    ).astype(np.float32)


def image_rows(a, b):
    out = np.zeros((COLS, COLS, 2 * WIDTH, 128), ml_dtypes.bfloat16)
    k = np.arange(WIDTH)
    for mine in range(COLS):
        r = WIDTH * mine + np.arange(WIDTH)
        for c in range(COLS):
            phase = np.exp(2j * np.pi * ((r[:, None] * (k + WIDTH * c)[None, :]) % ROWS) / ROWS)
            phase = phase / math.sqrt(ROWS)
            full = np.zeros((WIDTH, 64), complex)
            full[:, :WIDTH] = (phase * np.conj(b)[None, :])[:, ORDER]
            full[:, WIDTH] = phase @ np.conj(a)
            hi, lo = split_np(np.concatenate([full.real, full.imag], axis=0))
            out[mine, c, :, :64] = hi
            out[mine, c, :, 64:] = lo
    return out


def half_turn(cell):
    z = (cell - 128.0) * (math.pi / 256)
    w = z * z
    s = 1.0 / math.factorial(13)
    for n in (11, 9, 7, 5, 3, 1):
        s = s * w + (1.0 if n % 4 == 1 else -1.0) / math.factorial(n)
    c = 1.0 / math.factorial(12)
    for n in (10, 8, 6, 4, 2, 0):
        c = c * w + (1.0 if n % 4 == 0 else -1.0) / math.factorial(n)
    return jnp.where(cell == 0.0, 1e30, -(s * z) / c)


def ratio(cot, square, turn):
    return cot + square / (turn - cot)


def cotangent(cot, square, turn, kappa, cell3, threes):
    return jnp.where(threes, jnp.where(kappa == cell3, 1.0, 0.0), ratio(cot, square, turn))


def extract_kernel(
    offset_hbm, x_hbm, tw_hbm, f_hbm, out_ref, mid, spectrum, offset_ref, x_ref, tw_ref, f_ref, sem
):
    copies = [pltpu.make_async_copy(tw_hbm, tw_ref, sem.at[6])]
    for n in range(6):
        rows = pl.ds(8 * n, 8)
        copies.append(pltpu.make_async_copy(x_hbm.at[:, rows, :], x_ref.at[:, rows, :], sem.at[n]))
    copies.append(pltpu.make_async_copy(f_hbm, f_ref, sem.at[7]))
    copies.append(pltpu.make_async_copy(offset_hbm, offset_ref, sem.at[8]))
    for copy in copies:
        copy.start()
    mid[:, WIDTH:64, :] = jnp.zeros((16, 64 - WIDTH, 256), F32)
    copies[0].wait()
    for r in range(0, WIDTH, 8):
        copies[1 + r // 8].wait()
        xs = [
            (x_ref[0, r : r + 8, 128 * t : 128 * t + 128], x_ref[1, r : r + 8, 128 * t : 128 * t + 128])
            for t in range(16)
        ]
        ys = fft_list(xs, -1.0)
        for beta in range(16):
            yr, yi = ys[beta]
            c = tw_ref[0, beta : beta + 1, :]
            s = tw_ref[1, beta : beta + 1, :]
            mid[beta, r : r + 8, 0:128] = yr * c + yi * s
            mid[beta, r : r + 8, 128:256] = yi * c - yr * s
    copies[7].wait()
    copies[8].wait()
    left = (f_ref[0], f_ref[1])
    rights = []
    for beta in range(0, 16, 2):
        his, los = [], []
        for b in (beta, beta + 1):
            rh, rl = split(mid[b, :, 0:128])
            ih, il = split(mid[b, :, 128:256])
            his += [jnp.concatenate([rh, ih], axis=1), jnp.concatenate([ih, -rh], axis=1)]
            los += [jnp.concatenate([rl, il], axis=1), jnp.concatenate([il, -rl], axis=1)]
        rights.append((jnp.concatenate(his, axis=0), jnp.concatenate(los, axis=0)))
    freqs = [dot3(left, right, transposed=True) for right in rights]
    for beta in range(16):
        half = 128 * (beta % 2)
        spectrum[pl.ds(beta, 128, stride=16), :] = freqs[beta // 2][:, half : half + 128]
    spectrum[LENGTH:PADDED, :] = spectrum[0:WIDTH, :]
    column = lax.axis_index("col")
    for s in range(FACETS):
        out_ref[s] = spectrum[pl.ds(offset_ref[column, s], WIDTH), :]


def predict_kernel(k_ref, uv_ref, m_ref, rows_ref, coef_ref, res_ref, send_ref):
    uv = uv_ref[...].astype(F32)
    angles = half_turn(uv)
    iota = lax.broadcasted_iota(jnp.int32, (WIDTH, 128), 0)
    threes = iota % 3 == 0
    kap = iota.astype(F32)
    ar, ai, br, bi = (coef_ref[n] for n in range(4))
    zeros = jnp.zeros((16, 128), F32)

    mixes, others = [], []
    for f in range(FACETS):
        cot = rows_ref[f]
        square = 1.0 + cot * cot
        pr, pi = [], []
        for n in range(2):
            cell = 3.0 * uv[n : n + 1] - float(f * WIDTH)
            value = cotangent(cot, square, angles[n : n + 1], kap, cell, threes)
            pr.append(ar + br * value)
            pi.append(ai + bi * value)
        left = jnp.concatenate([pr[0], zeros, -pi[0], zeros], axis=0)
        right = jnp.concatenate([pi[0], zeros, pr[0], zeros], axis=0)
        mixes.append(split(jnp.concatenate([left, right], axis=1)))
        others.append((pr[1], pi[1]))
    sums = [dot3(split(k_ref[f]), mixes[f]) for f in range(FACETS)]
    sr = jnp.zeros((WIDTH, 128), F32)
    si = jnp.zeros((WIDTH, 128), F32)
    for f in range(FACETS):
        tr, ti = sums[f][:, :128], sums[f][:, 128:]
        pr, pi = others[f]
        sr = sr + (tr * pr - ti * pi)
        si = si + (tr * pi + ti * pr)
    res = jnp.concatenate(
        [
            m_ref[0:1] - jnp.sum(sr, axis=0, keepdims=True) * (1.0 / SUBGRID),
            m_ref[1:2] - jnp.sum(si, axis=0, keepdims=True) * (1.0 / SUBGRID),
        ],
        axis=0,
    )
    res_ref[...] = res
    send_ref[...] = jnp.broadcast_to(
        jnp.concatenate([res, uv], axis=0)[None], (FACETS * COLS, 4, 128)
    )


def image_kernel(
    offset_hbm, got_ref, live_ref, gamma_ref, tw_ref, b_ref, out_hbm, grid, mid, out_ref, offset_ref, sem
):
    fetch = pltpu.make_async_copy(offset_hbm, offset_ref, sem.at[6])
    fetch.start()
    facet, column = lax.axis_index("facet"), lax.axis_index("col")
    grid[...] = jnp.zeros((3, PADDED, 128), F32)
    iota = lax.broadcasted_iota(jnp.int32, (16, 128), 0)
    kap = (iota + 16 * facet).astype(F32)
    cot = live_ref[facet]
    square = 1.0 + cot * cot
    one_h = jnp.where(iota == 0, 1.0, 0.0).astype(BF16)
    none_h = jnp.zeros((32, 128), BF16)
    pad = jnp.zeros((64 - WIDTH, 128), F32)
    lanes = lax.broadcasted_iota(jnp.int32, (1, 128), 1)
    turn = jnp.where(lanes < 64, -1.0, 1.0)

    def parts(angle, cell):
        hi, lo = split(ratio(cot, square, angle))
        hit = jnp.where(kap == cell, 1.0, 0.0).astype(BF16)
        return jnp.concatenate([hi, hit, one_h], axis=0), lo

    fetch.wait()

    def step(g, carry):
        first = g * (GROUP // FACETS)
        gots, turns = [], []
        for n in range(GROUP):
            got = got_ref[g * GROUP + n]
            angles = half_turn(got)
            gots.append([got[r : r + 1] for r in range(4)])
            turns.append([angles[r : r + 1] for r in (2, 3)])
        gs, vs, hs = {}, {}, {}

        def gamma(n):
            gam = gamma_ref[column, first + n // FACETS]
            return jnp.concatenate([gam, gam[:, :32]], axis=1)

        def rows_of(n):
            h, l = parts(turns[n][0], gots[n][2])
            gs[n] = dot(gamma(n), jnp.concatenate([h, h, l], axis=0))
            vs[n] = parts(turns[n][1], gots[n][3])

        def columns_of(n):
            rr, ri = gots[n][0], gots[n][1]
            gr, gi = gs[n][:WIDTH], gs[n][WIDTH:]
            w = jnp.concatenate([gr * rr - gi * ri, pad, gr * ri + gi * rr, pad], axis=0)
            wh, wl = split(w)
            vh, vl = vs[n]
            left = jnp.concatenate(
                [jnp.concatenate([vh, vh], axis=1), jnp.concatenate([vl, none_h], axis=1)], axis=0
            )
            hs[n] = dot(left, jnp.concatenate([wh, wl], axis=1), transposed=True)

        def place(n):
            h = hs[n]
            total = turn * pltpu.roll(h[WIDTH : WIDTH + 1], 64, 1)
            o = offset_ref[first + n // FACETS, n % FACETS]
            for m in range(3):
                add = h[16 * m : 16 * m + 16]
                if m < 2:
                    add = add + h[64 + 16 * m : 80 + 16 * m] + total
                at = pl.ds(o + (m + 1) % 3, 16, stride=3)
                grid[m, at, :] = grid[m, at, :] + add

        for n in range(GROUP + LAG2):
            for fn, lag in ((rows_of, 0), (columns_of, LAG1), (place, LAG2)):
                if 0 <= n - lag < GROUP:
                    fn(n - lag)
        return carry

    lax.fori_loop(0, FACETS * COLS // GROUP, step, 0)
    grid[:, 0:WIDTH, :] = grid[:, 0:WIDTH, :] + grid[:, LENGTH:PADDED, :]
    q = float(FACETS * WIDTH * WIDTH) ** (-0.25)
    right = (b_ref[0], b_ref[1])
    lefts = []
    for beta in range(16):
        one, two, nil = (grid[m, pl.ds(beta, 128, stride=16), :] for m in range(3))
        d = (SUBGRID * q) * nil + (q * math.sqrt(3) / 4) * (one - two)
        d = (d - (0.75 * q) * turn * pltpu.roll(one + two, 64, 1)).T
        lefts.append(split(jnp.concatenate([d[0:WIDTH], d[64 : 64 + WIDTH]], axis=1)))
    freqs = [dot3(left, right) for left in lefts]
    for beta in range(16):
        yr, yi = freqs[beta][:, :128], freqs[beta][:, 128:]
        c = tw_ref[0, beta : beta + 1, :]
        s = tw_ref[1, beta : beta + 1, :]
        mid[beta, :, 0:128] = yr * c - yi * s
        mid[beta, :, 128:256] = yi * c + yr * s
    copies = []
    for r in range(0, WIDTH, 8):
        ys = fft_list(
            [(mid[b, r : r + 8, 0:128], mid[b, r : r + 8, 128:256]) for b in range(16)], 1.0
        )
        for t in range(16):
            out_ref[0, r : r + 8, 128 * t : 128 * t + 128] = ys[t][0]
            out_ref[1, r : r + 8, 128 * t : 128 * t + 128] = ys[t][1]
        rows = pl.ds(r, 8)
        copies.append(
            pltpu.make_async_copy(out_ref.at[:, rows, :], out_hbm.at[:, rows, :], sem.at[r // 8])
        )
        copies[-1].start()
    for copy in copies:
        copy.wait()


def keep(x):
    return pltpu.with_memory_space_constraint(x, pltpu.MemorySpace.HBM)


def params():
    return pltpu.CompilerParams(vmem_limit_bytes=48 << 20)


VM = pltpu.MemorySpace.VMEM


def solution(mesh):
    twiddle, forward, backward, rows, live, a, b = tables()
    coef = row_coefficients(a, b)
    gamma = image_rows(a, b)

    def body(strips, sub_offset, uv_cells, measured):
        vm = pl.BlockSpec(memory_space=VM)
        hbm = pl.BlockSpec(memory_space=pltpu.MemorySpace.HBM)
        windows = pl.pallas_call(
            extract_kernel,
            out_shape=jax.ShapeDtypeStruct((FACETS, WIDTH, 128), F32),
            in_specs=[hbm, hbm, hbm, hbm],
            out_specs=vm,
            scratch_shapes=[
                pltpu.VMEM((16, 64, 256), F32),
                pltpu.VMEM((PADDED, 128), F32),
                pltpu.SMEM((COLS, FACETS), jnp.int32),
                pltpu.VMEM((2, WIDTH, LENGTH), F32),
                pltpu.VMEM((2, 16, 128), F32),
                pltpu.VMEM((2, 128, 256), BF16),
                pltpu.SemaphoreType.DMA((9,)),
            ],
            compiler_params=params(),
            name="extract",
        )(*(keep(x) for x in (sub_offset, strips[0], jnp.asarray(twiddle), jnp.asarray(forward))))
        arrived = lax.all_to_all(windows, "facet", split_axis=0, concat_axis=0, tiled=True)
        res, send = pl.pallas_call(
            predict_kernel,
            out_shape=(
                jax.ShapeDtypeStruct((2, 128), F32),
                jax.ShapeDtypeStruct((FACETS * COLS, 4, 128), F32),
            ),
            in_specs=[vm] * 5,
            out_specs=(vm, vm),
            compiler_params=params(),
            name="predict",
        )(arrived, uv_cells[0, 0], measured[0, 0], jnp.asarray(rows), jnp.asarray(coef))
        got = lax.all_to_all(send, ("col", "facet"), split_axis=0, concat_axis=0, tiled=True)
        image = pl.pallas_call(
            image_kernel,
            out_shape=jax.ShapeDtypeStruct((2, WIDTH, LENGTH), F32),
            in_specs=[hbm, vm, vm, vm, vm, vm],
            out_specs=pl.BlockSpec(memory_space=pl.ANY),
            scratch_shapes=[
                pltpu.VMEM((3, PADDED, 128), F32),
                pltpu.VMEM((16, WIDTH, 256), F32),
                pltpu.VMEM((2, WIDTH, LENGTH), F32),
                pltpu.SMEM((COLS, FACETS), jnp.int32),
                pltpu.SemaphoreType.DMA((7,)),
            ],
            compiler_params=params(),
            name="image",
        )(
            keep(sub_offset),
            got,
            jnp.asarray(live),
            jnp.asarray(gamma),
            jnp.asarray(twiddle),
            jnp.asarray(backward),
        )
        return image[None], res[None, None]

    return jax.shard_map(
        body,
        mesh=mesh,
        in_specs=(
            P("facet", None, "col", None),
            P(),
            P("col", "facet", None, None),
            P("col", "facet", None, None),
        ),
        out_specs=(P("facet", None, "col", None), P("col", "facet", None, None)),
        check_vma=False,
    )
```

```python
import math

import jax
import jax.numpy as jnp
import ml_dtypes
import numpy as np
from jax import lax
from jax.experimental import pallas as pl
from jax.experimental.pallas import tpu as pltpu
from jax.sharding import PartitionSpec as P

SUBGRID = 256
WIDTH = 48
SENT = 40
LENGTH = 2048
FACETS = 16
COLS = 8
GROUP = 128
LAG1 = 8
LAG2 = 16
ROWS = 384
PADDED = LENGTH + WIDTH
TOTAL = FACETS * WIDTH
F32 = jnp.float32
BF16 = jnp.bfloat16
ORDER = np.concatenate([np.arange(1, WIDTH, 3), np.arange(2, WIDTH, 3), np.arange(0, WIDTH, 3)])


def split_np(x):
    x = np.asarray(x, np.float32)
    hi = x.astype(ml_dtypes.bfloat16)
    lo = (x - hi.astype(np.float32)).astype(ml_dtypes.bfloat16)
    return hi, lo


def split(x):
    hi = x.astype(BF16)
    lo = (x - hi.astype(F32)).astype(BF16)
    return hi, lo


def dot(a, b, transposed=False):
    dims = (((1,), (1 if transposed else 0,)), ((), ()))
    return lax.dot_general(a, b, dims, preferred_element_type=F32)


def dot3(a, b, transposed=False):
    (ah, al), (bh, bl) = a, b
    rows = ah.shape[0]
    both = dot(jnp.concatenate([ah, al], axis=0), bh, transposed)
    return both[:rows] + both[rows:] + dot(ah, bl, transposed)


def fft_list(xs, sign):
    n = len(xs)
    if n == 1:
        return xs
    even = fft_list(xs[0::2], sign)
    odd = fft_list(xs[1::2], sign)
    half = n // 2
    out = [None] * n
    for k in range(half):
        (er, ei), (r, i) = even[k], odd[k]
        if k == 0:
            tr, ti = r, i
        elif 4 * k == n:
            tr, ti = -sign * i, sign * r
        elif 8 * k == n:
            h = math.sqrt(0.5)
            tr, ti = h * (r - sign * i), h * (i + sign * r)
        elif 8 * k == 3 * n:
            h = math.sqrt(0.5)
            tr, ti = -h * (r + sign * i), h * (sign * r - i)
        else:
            c = math.cos(2 * math.pi * k / n)
            s = sign * math.sin(2 * math.pi * k / n)
            tr, ti = c * r - s * i, s * r + c * i
        out[k] = (er + tr, ei + ti)
        out[k + half] = (er - tr, ei - ti)
    return out


def tables():
    lane = np.arange(128)
    beta = np.arange(16)[:, None]
    ang = 2 * np.pi * ((lane[None, :] * beta) % LENGTH) / LENGTH
    norm = 1 / math.sqrt(LENGTH)
    twiddle = (np.stack([np.cos(ang), np.sin(ang)]) * norm).astype(np.float32)
    ang = 2 * np.pi * ((lane[:, None] * lane[None, :]) % 128) / 128
    cos, sin = np.cos(ang), np.sin(ang)
    forward = np.stack(split_np(np.concatenate([cos, sin], axis=1)))
    backward = np.stack(
        split_np(
            np.concatenate(
                [np.concatenate([cos, sin], axis=1), np.concatenate([-sin, cos], axis=1)], axis=0
            )
        )
    )
    kappa = np.arange(TOTAL).reshape(FACETS, WIDTH, 1) * np.ones((1, 1, 128))
    angle = np.pi * kappa / TOTAL
    cot = np.where(kappa % 3 == 0, 0.0, 1 / np.tan(np.where(kappa % 3 == 0, 1.0, angle)))
    rows = cot.astype(np.float32)
    live = np.ascontiguousarray(rows[:, ORDER[:32]])
    q = float(FACETS * WIDTH * WIDTH) ** (-0.25)
    k = np.arange(WIDTH)
    numer = np.exp(2j * np.pi * (k % 3) / 3) - 1
    a = np.where(k % 3 == 0, 0, -0.5 * q * numer)
    b = np.where(k % 3 == 0, SUBGRID * q, -0.5j * q * numer)
    return twiddle, forward, backward, rows, live, a, b


def row_coefficients(a, b):
    return np.stack(
        [np.broadcast_to(v[:, None], (WIDTH, 128)) for v in (a.real, a.imag, b.real, b.imag)]
    ).astype(np.float32)


def image_rows(a, b):
    out = np.zeros((COLS, COLS, 2 * WIDTH, 128), ml_dtypes.bfloat16)
    k = np.arange(WIDTH)
    for mine in range(COLS):
        r = WIDTH * mine + np.arange(WIDTH)
        for c in range(COLS):
            phase = np.exp(2j * np.pi * ((r[:, None] * (k + WIDTH * c)[None, :]) % ROWS) / ROWS)
            phase = phase / math.sqrt(ROWS)
            full = np.zeros((WIDTH, 64), complex)
            full[:, :WIDTH] = (phase * np.conj(b)[None, :])[:, ORDER]
            full[:, WIDTH] = phase @ np.conj(a)
            hi, lo = split_np(np.concatenate([full.real, full.imag], axis=0))
            out[mine, c, :, :64] = hi
            out[mine, c, :, 64:] = lo
    return out


def half_turn(cell):
    z = (cell - 128.0) * (math.pi / 256)
    w = z * z
    s = 1.0 / math.factorial(13)
    for n in (11, 9, 7, 5, 3, 1):
        s = s * w + (1.0 if n % 4 == 1 else -1.0) / math.factorial(n)
    c = 1.0 / math.factorial(12)
    for n in (10, 8, 6, 4, 2, 0):
        c = c * w + (1.0 if n % 4 == 0 else -1.0) / math.factorial(n)
    return jnp.where(cell == 0.0, 1e30, -(s * z) / c)


def ratio(cot, square, turn):
    return cot + square / (turn - cot)


def cotangent(cot, square, turn, kappa, cell3, threes):
    return jnp.where(threes, jnp.where(kappa == cell3, 1.0, 0.0), ratio(cot, square, turn))


def extract_kernel(
    offset_hbm, x_hbm, tw_hbm, f_hbm, out_ref, mid, spectrum, offset_ref, x_ref, tw_ref, f_ref, sem
):
    copies = [pltpu.make_async_copy(tw_hbm, tw_ref, sem.at[6])]
    for n in range(6):
        rows = pl.ds(8 * n, 8)
        copies.append(pltpu.make_async_copy(x_hbm.at[:, rows, :], x_ref.at[:, rows, :], sem.at[n]))
    copies.append(pltpu.make_async_copy(f_hbm, f_ref, sem.at[7]))
    copies.append(pltpu.make_async_copy(offset_hbm, offset_ref, sem.at[8]))
    for copy in copies:
        copy.start()
    copies[0].wait()
    for r in range(0, WIDTH, 8):
        copies[1 + r // 8].wait()
        xs = [
            (x_ref[0, r : r + 8, 128 * t : 128 * t + 128], x_ref[1, r : r + 8, 128 * t : 128 * t + 128])
            for t in range(16)
        ]
        ys = fft_list(xs, -1.0)
        for beta in range(16):
            yr, yi = ys[beta]
            c = tw_ref[0, beta : beta + 1, :]
            s = tw_ref[1, beta : beta + 1, :]
            mid[beta, r : r + 8, 0:128] = yr * c + yi * s
            mid[beta, r : r + 8, 128:256] = yi * c - yr * s
    copies[7].wait()
    copies[8].wait()
    left = (f_ref[0], f_ref[1])
    none = jnp.zeros((128 - 2 * WIDTH, 256), BF16)
    rights = []
    for beta in range(0, 16, 2):
        his, los = [], []
        for b in (beta, beta + 1):
            rh, rl = split(mid[b, :, 0:128])
            ih, il = split(mid[b, :, 128:256])
            his += [jnp.concatenate([rh, ih], axis=1), jnp.concatenate([ih, -rh], axis=1), none]
            los += [jnp.concatenate([rl, il], axis=1), jnp.concatenate([il, -rl], axis=1), none]
        rights.append((jnp.concatenate(his, axis=0), jnp.concatenate(los, axis=0)))
    freqs = [dot3(left, right, transposed=True) for right in rights]
    for beta in range(16):
        half = 128 * (beta % 2)
        spectrum[pl.ds(beta, 128, stride=16), :] = freqs[beta // 2][:, half : half + 128]
    spectrum[LENGTH:PADDED, :] = spectrum[0:WIDTH, :]
    column = lax.axis_index("col")
    free = lax.broadcasted_iota(jnp.int32, (8, 128), 1) >= 96
    for s in range(FACETS):
        o = offset_ref[column, s]
        tail = spectrum[pl.ds(o + SENT, WIDTH - SENT), :]
        for n in range(SENT // 8):
            rows = spectrum[pl.ds(o + 8 * n, 8), :]
            if n < 3:
                rows = jnp.where(free, pltpu.roll(tail, 96 - 32 * n, 1), rows)
            out_ref[s, 8 * n : 8 * n + 8, :] = rows


def predict_kernel(k_ref, uv_ref, m_ref, rows_ref, coef_ref, res_ref, send_ref):
    uv = uv_ref[...].astype(F32)
    angles = half_turn(uv)
    iota = lax.broadcasted_iota(jnp.int32, (WIDTH, 128), 0)
    threes = iota % 3 == 0
    kap = iota.astype(F32)
    ar, ai, br, bi = (coef_ref[n] for n in range(4))
    zeros = jnp.zeros((128 - 2 * WIDTH, 128), F32)
    lane = lax.broadcasted_iota(jnp.int32, (8, 128), 1)

    def unpack(f):
        tail = pltpu.roll(k_ref[f, 0:8, :], 32, 1)
        for n in (1, 2):
            piece = pltpu.roll(k_ref[f, 8 * n : 8 * n + 8, :], 32 * n + 32, 1)
            tail = jnp.where(lane < 32 * n, tail, piece)
        return split(jnp.concatenate([k_ref[f], tail], axis=0))


    mixes, others = [], []
    for f in range(FACETS):
        cot = rows_ref[f]
        square = 1.0 + cot * cot
        pr, pi = [], []
        for n in range(2):
            cell = 3.0 * uv[n : n + 1] - float(f * WIDTH)
            value = cotangent(cot, square, angles[n : n + 1], kap, cell, threes)
            pr.append(ar + br * value)
            pi.append(ai + bi * value)
        left = jnp.concatenate([pr[0], -pi[0], zeros], axis=0)
        right = jnp.concatenate([pi[0], pr[0], zeros], axis=0)
        mixes.append(split(jnp.concatenate([left, right], axis=1)))
        others.append((pr[1], pi[1]))
    sums = [dot3(unpack(f), mixes[f]) for f in range(FACETS)]
    sr = jnp.zeros((WIDTH, 128), F32)
    si = jnp.zeros((WIDTH, 128), F32)
    for f in range(FACETS):
        tr, ti = sums[f][:, :128], sums[f][:, 128:]
        pr, pi = others[f]
        sr = sr + (tr * pr - ti * pi)
        si = si + (tr * pi + ti * pr)
    res = jnp.concatenate(
        [
            m_ref[0:1] - jnp.sum(sr, axis=0, keepdims=True) * (1.0 / SUBGRID),
            m_ref[1:2] - jnp.sum(si, axis=0, keepdims=True) * (1.0 / SUBGRID),
        ],
        axis=0,
    )
    res_ref[...] = res
    send_ref[...] = jnp.broadcast_to(
        jnp.concatenate([res, uv], axis=0)[None], (FACETS * COLS, 4, 128)
    )


def image_kernel(
    offset_hbm, got_ref, live_ref, gamma_ref, tw_ref, b_ref, out_hbm, grid, mid, out_ref, offset_ref, sem
):
    fetch = pltpu.make_async_copy(offset_hbm, offset_ref, sem.at[6])
    fetch.start()
    facet, column = lax.axis_index("facet"), lax.axis_index("col")
    grid[...] = jnp.zeros((3, PADDED, 128), F32)
    iota = lax.broadcasted_iota(jnp.int32, (16, 128), 0)
    kap = (iota + 16 * facet).astype(F32)
    cot = live_ref[facet]
    square = 1.0 + cot * cot
    one_h = jnp.where(iota == 0, 1.0, 0.0).astype(BF16)
    none_h = jnp.zeros((32, 128), BF16)
    pad = jnp.zeros((64 - WIDTH, 128), F32)
    lanes = lax.broadcasted_iota(jnp.int32, (1, 128), 1)
    turn = jnp.where(lanes < 64, -1.0, 1.0)

    def parts(angle, cell):
        hi, lo = split(ratio(cot, square, angle))
        hit = jnp.where(kap == cell, 1.0, 0.0).astype(BF16)
        return jnp.concatenate([hi, hit, one_h], axis=0), lo

    fetch.wait()

    def step(g, carry):
        first = g * (GROUP // FACETS)
        gots, turns = [], []
        for n in range(GROUP):
            got = got_ref[g * GROUP + n]
            angles = half_turn(got)
            gots.append([got[r : r + 1] for r in range(4)])
            turns.append([angles[r : r + 1] for r in (2, 3)])
        gs, vs, hs = {}, {}, {}

        def gamma(n):
            gam = gamma_ref[column, first + n // FACETS]
            return jnp.concatenate([gam, gam[:, :32]], axis=1)

        def rows_of(n):
            h, l = parts(turns[n][0], gots[n][2])
            gs[n] = dot(gamma(n), jnp.concatenate([h, h, l], axis=0))
            vs[n] = parts(turns[n][1], gots[n][3])

        def columns_of(n):
            rr, ri = gots[n][0], gots[n][1]
            gr, gi = gs[n][:WIDTH], gs[n][WIDTH:]
            w = jnp.concatenate([gr * rr - gi * ri, pad, gr * ri + gi * rr, pad], axis=0)
            wh, wl = split(w)
            vh, vl = vs[n]
            left = jnp.concatenate(
                [jnp.concatenate([vh, vh], axis=1), jnp.concatenate([vl, none_h], axis=1)], axis=0
            )
            hs[n] = dot(left, jnp.concatenate([wh, wl], axis=1), transposed=True)

        def place(n):
            h = hs[n]
            total = turn * pltpu.roll(h[WIDTH : WIDTH + 1], 64, 1)
            o = offset_ref[first + n // FACETS, n % FACETS]
            for m in range(3):
                add = h[16 * m : 16 * m + 16]
                if m < 2:
                    add = add + h[64 + 16 * m : 80 + 16 * m] + total
                at = pl.ds(o + (m + 1) % 3, 16, stride=3)
                grid[m, at, :] = grid[m, at, :] + add

        for n in range(GROUP + LAG2):
            for fn, lag in ((rows_of, 0), (columns_of, LAG1), (place, LAG2)):
                if 0 <= n - lag < GROUP:
                    fn(n - lag)
        return carry

    lax.fori_loop(0, FACETS * COLS // GROUP, step, 0)
    grid[:, 0:WIDTH, :] = grid[:, 0:WIDTH, :] + grid[:, LENGTH:PADDED, :]
    q = float(FACETS * WIDTH * WIDTH) ** (-0.25)
    for row in range(0, LENGTH, 64):
        one, two, nil = (grid[m, row : row + 64, :] for m in range(3))
        d = (SUBGRID * q) * nil + (q * math.sqrt(3) / 4) * (one - two)
        grid[2, row : row + 64, :] = d - (0.75 * q) * turn * pltpu.roll(one + two, 64, 1)
    right = (b_ref[0], b_ref[1])
    lefts = []
    for beta in range(16):
        d = grid[2, pl.ds(beta, 128, stride=16), :].T
        lefts.append(split(jnp.concatenate([d[0:WIDTH], d[64 : 64 + WIDTH]], axis=1)))
    freqs = [dot3(left, right) for left in lefts]
    for beta in range(16):
        yr, yi = freqs[beta][:, :128], freqs[beta][:, 128:]
        c = tw_ref[0, beta : beta + 1, :]
        s = tw_ref[1, beta : beta + 1, :]
        mid[beta, :, 0:128] = yr * c - yi * s
        mid[beta, :, 128:256] = yi * c + yr * s
    copies = []
    for r in range(0, WIDTH, 8):
        ys = fft_list(
            [(mid[b, r : r + 8, 0:128], mid[b, r : r + 8, 128:256]) for b in range(16)], 1.0
        )
        for t in range(16):
            out_ref[0, r : r + 8, 128 * t : 128 * t + 128] = ys[t][0]
            out_ref[1, r : r + 8, 128 * t : 128 * t + 128] = ys[t][1]
        rows = pl.ds(r, 8)
        copies.append(
            pltpu.make_async_copy(out_ref.at[:, rows, :], out_hbm.at[:, rows, :], sem.at[r // 8])
        )
        copies[-1].start()
    for copy in copies:
        copy.wait()


def keep(x):
    return pltpu.with_memory_space_constraint(x, pltpu.MemorySpace.HBM)


def params():
    return pltpu.CompilerParams(vmem_limit_bytes=48 << 20)


VM = pltpu.MemorySpace.VMEM


def solution(mesh):
    twiddle, forward, backward, rows, live, a, b = tables()
    coef = row_coefficients(a, b)
    gamma = image_rows(a, b)

    def body(strips, sub_offset, uv_cells, measured):
        vm = pl.BlockSpec(memory_space=VM)
        hbm = pl.BlockSpec(memory_space=pltpu.MemorySpace.HBM)
        windows = pl.pallas_call(
            extract_kernel,
            out_shape=jax.ShapeDtypeStruct((FACETS, SENT, 128), F32),
            in_specs=[hbm, hbm, hbm, hbm],
            out_specs=vm,
            scratch_shapes=[
                pltpu.VMEM((16, WIDTH, 256), F32),
                pltpu.VMEM((PADDED, 128), F32),
                pltpu.SMEM((COLS, FACETS), jnp.int32),
                pltpu.VMEM((2, WIDTH, LENGTH), F32),
                pltpu.VMEM((2, 16, 128), F32),
                pltpu.VMEM((2, 128, 256), BF16),
                pltpu.SemaphoreType.DMA((9,)),
            ],
            compiler_params=params(),
            name="extract",
        )(*(keep(x) for x in (sub_offset, strips[0], jnp.asarray(twiddle), jnp.asarray(forward))))
        arrived = lax.all_to_all(windows, "facet", split_axis=0, concat_axis=0, tiled=True)
        res, send = pl.pallas_call(
            predict_kernel,
            out_shape=(
                jax.ShapeDtypeStruct((2, 128), F32),
                jax.ShapeDtypeStruct((FACETS * COLS, 4, 128), F32),
            ),
            in_specs=[vm] * 5,
            out_specs=(vm, vm),
            compiler_params=params(),
            name="predict",
        )(arrived, uv_cells[0, 0], measured[0, 0], jnp.asarray(rows), jnp.asarray(coef))
        got = lax.all_to_all(send, ("col", "facet"), split_axis=0, concat_axis=0, tiled=True)
        image = pl.pallas_call(
            image_kernel,
            out_shape=jax.ShapeDtypeStruct((2, WIDTH, LENGTH), F32),
            in_specs=[hbm, vm, vm, vm, vm, vm],
            out_specs=pl.BlockSpec(memory_space=pl.ANY),
            scratch_shapes=[
                pltpu.VMEM((3, PADDED, 128), F32),
                pltpu.VMEM((16, WIDTH, 256), F32),
                pltpu.VMEM((2, WIDTH, LENGTH), F32),
                pltpu.SMEM((COLS, FACETS), jnp.int32),
                pltpu.SemaphoreType.DMA((7,)),
            ],
            compiler_params=params(),
            name="image",
        )(
            keep(sub_offset),
            got,
            jnp.asarray(live),
            jnp.asarray(gamma),
            jnp.asarray(twiddle),
            jnp.asarray(backward),
        )
        return image[None], res[None, None]

    return jax.shard_map(
        body,
        mesh=mesh,
        in_specs=(
            P("facet", None, "col", None),
            P(),
            P("col", "facet", None, None),
            P("col", "facet", None, None),
        ),
        out_specs=(P("facet", None, "col", None), P("col", "facet", None, None)),
        check_vma=False,
    )
```

```python
import math

import jax
import jax.numpy as jnp
import ml_dtypes
import numpy as np
from jax import lax
from jax.experimental import pallas as pl
from jax.experimental.pallas import tpu as pltpu
from jax.sharding import PartitionSpec as P

SUBGRID = 256
WIDTH = 48
SENT = 40
LENGTH = 2048
FACETS = 16
COLS = 8
GROUP = 128
LAG1 = 8
LAG2 = 16
ROWS = 384
PADDED = LENGTH + WIDTH
TOTAL = FACETS * WIDTH
F32 = jnp.float32
BF16 = jnp.bfloat16
ORDER = np.concatenate([np.arange(1, WIDTH, 3), np.arange(2, WIDTH, 3), np.arange(0, WIDTH, 3)])


def split_np(x):
    x = np.asarray(x, np.float32)
    hi = x.astype(ml_dtypes.bfloat16)
    lo = (x - hi.astype(np.float32)).astype(ml_dtypes.bfloat16)
    return hi, lo


def split(x):
    hi = x.astype(BF16)
    lo = (x - hi.astype(F32)).astype(BF16)
    return hi, lo


def dot(a, b, transposed=False):
    dims = (((1,), (1 if transposed else 0,)), ((), ()))
    return lax.dot_general(a, b, dims, preferred_element_type=F32)


def dot3(a, b, transposed=False):
    (ah, al), (bh, bl) = a, b
    rows = ah.shape[0]
    both = dot(jnp.concatenate([ah, al], axis=0), bh, transposed)
    return both[:rows] + both[rows:] + dot(ah, bl, transposed)


def fft_list(xs, sign):
    n = len(xs)
    if n == 1:
        return xs
    even = fft_list(xs[0::2], sign)
    odd = fft_list(xs[1::2], sign)
    half = n // 2
    out = [None] * n
    for k in range(half):
        (er, ei), (r, i) = even[k], odd[k]
        if k == 0:
            tr, ti = r, i
        elif 4 * k == n:
            tr, ti = -sign * i, sign * r
        elif 8 * k == n:
            h = math.sqrt(0.5)
            tr, ti = h * (r - sign * i), h * (i + sign * r)
        elif 8 * k == 3 * n:
            h = math.sqrt(0.5)
            tr, ti = -h * (r + sign * i), h * (sign * r - i)
        else:
            c = math.cos(2 * math.pi * k / n)
            s = sign * math.sin(2 * math.pi * k / n)
            tr, ti = c * r - s * i, s * r + c * i
        out[k] = (er + tr, ei + ti)
        out[k + half] = (er - tr, ei - ti)
    return out


def tables():
    lane = np.arange(128)
    beta = np.arange(16)[:, None]
    ang = 2 * np.pi * ((lane[None, :] * beta) % LENGTH) / LENGTH
    norm = 1 / math.sqrt(LENGTH)
    twiddle = (np.stack([np.cos(ang), np.sin(ang)]) * norm).astype(np.float32)
    ang = 2 * np.pi * ((lane[:, None] * lane[None, :]) % 128) / 128
    cos, sin = np.cos(ang), np.sin(ang)
    forward = np.stack(split_np(np.concatenate([cos, sin], axis=1)))
    backward = np.stack(
        split_np(
            np.concatenate(
                [np.concatenate([cos, sin], axis=1), np.concatenate([-sin, cos], axis=1)], axis=0
            )
        )
    )
    kappa = np.arange(TOTAL).reshape(FACETS, WIDTH, 1) * np.ones((1, 1, 128))
    angle = np.pi * kappa / TOTAL
    cot = np.where(kappa % 3 == 0, 0.0, 1 / np.tan(np.where(kappa % 3 == 0, 1.0, angle)))
    rows = cot.astype(np.float32)
    live = np.ascontiguousarray(rows[:, ORDER[:32]])
    q = float(FACETS * WIDTH * WIDTH) ** (-0.25)
    k = np.arange(WIDTH)
    numer = np.exp(2j * np.pi * (k % 3) / 3) - 1
    a = np.where(k % 3 == 0, 0, -0.5 * q * numer)
    b = np.where(k % 3 == 0, SUBGRID * q, -0.5j * q * numer)
    return twiddle, forward, backward, rows, live, a, b


def row_coefficients(a, b):
    return np.stack(
        [np.broadcast_to(v[:, None], (WIDTH, 128)) for v in (a.real, a.imag, b.real, b.imag)]
    ).astype(np.float32)


def image_rows(a, b):
    out = np.zeros((COLS, COLS, 2 * WIDTH, 128), ml_dtypes.bfloat16)
    k = np.arange(WIDTH)
    for mine in range(COLS):
        r = WIDTH * mine + np.arange(WIDTH)
        for c in range(COLS):
            phase = np.exp(2j * np.pi * ((r[:, None] * (k + WIDTH * c)[None, :]) % ROWS) / ROWS)
            phase = phase / math.sqrt(ROWS)
            full = np.zeros((WIDTH, 64), complex)
            full[:, :WIDTH] = (phase * np.conj(b)[None, :])[:, ORDER]
            full[:, WIDTH] = phase @ np.conj(a)
            hi, lo = split_np(np.concatenate([full.real, full.imag], axis=0))
            out[mine, c, :, :64] = hi
            out[mine, c, :, 64:] = lo
    return out


def half_turn(cell):
    z = (cell - 128.0) * (math.pi / 256)
    w = z * z
    s = 1.0 / math.factorial(13)
    for n in (11, 9, 7, 5, 3, 1):
        s = s * w + (1.0 if n % 4 == 1 else -1.0) / math.factorial(n)
    c = 1.0 / math.factorial(12)
    for n in (10, 8, 6, 4, 2, 0):
        c = c * w + (1.0 if n % 4 == 0 else -1.0) / math.factorial(n)
    return jnp.where(cell == 0.0, 1e30, -(s * z) / c)


def ratio(cot, square, turn):
    return cot + square / (turn - cot)


def cotangent(cot, square, turn, kappa, cell3, threes):
    return jnp.where(threes, jnp.where(kappa == cell3, 1.0, 0.0), ratio(cot, square, turn))


def extract_kernel(
    offset_hbm, x_hbm, tw_hbm, f_hbm, out_ref, mid, spectrum, offset_ref, x_ref, tw_ref, f_ref, sem
):
    copies = [pltpu.make_async_copy(tw_hbm, tw_ref, sem.at[6])]
    for n in range(6):
        rows = pl.ds(8 * n, 8)
        copies.append(pltpu.make_async_copy(x_hbm.at[:, rows, :], x_ref.at[:, rows, :], sem.at[n]))
    copies.append(pltpu.make_async_copy(f_hbm, f_ref, sem.at[7]))
    copies.append(pltpu.make_async_copy(offset_hbm, offset_ref, sem.at[8]))
    for copy in copies:
        copy.start()
    copies[0].wait()
    for r in range(0, WIDTH, 8):
        copies[1 + r // 8].wait()
        xs = [
            (x_ref[0, r : r + 8, 128 * t : 128 * t + 128], x_ref[1, r : r + 8, 128 * t : 128 * t + 128])
            for t in range(16)
        ]
        ys = fft_list(xs, -1.0)
        for beta in range(16):
            yr, yi = ys[beta]
            c = tw_ref[0, beta : beta + 1, :]
            s = tw_ref[1, beta : beta + 1, :]
            mid[beta, r : r + 8, 0:128] = yr * c + yi * s
            mid[beta, r : r + 8, 128:256] = yi * c - yr * s
    copies[7].wait()
    copies[8].wait()
    left = (f_ref[0], f_ref[1])
    none = jnp.zeros((128 - 2 * WIDTH, 256), BF16)
    rights = []
    for beta in range(0, 16, 2):
        his, los = [], []
        for b in (beta, beta + 1):
            rh, rl = split(mid[b, :, 0:128])
            ih, il = split(mid[b, :, 128:256])
            his += [jnp.concatenate([rh, ih], axis=1), jnp.concatenate([ih, -rh], axis=1), none]
            los += [jnp.concatenate([rl, il], axis=1), jnp.concatenate([il, -rl], axis=1), none]
        rights.append((jnp.concatenate(his, axis=0), jnp.concatenate(los, axis=0)))
    freqs = [dot3(left, right, transposed=True) for right in rights]
    for beta in range(16):
        half = 128 * (beta % 2)
        spectrum[pl.ds(beta, 128, stride=16), :] = freqs[beta // 2][:, half : half + 128]
    spectrum[LENGTH:PADDED, :] = spectrum[0:WIDTH, :]
    column = lax.axis_index("col")
    free = lax.broadcasted_iota(jnp.int32, (8, 128), 1) >= 96
    for s in range(FACETS):
        o = offset_ref[column, s]
        tail = spectrum[pl.ds(o + SENT, WIDTH - SENT), :]
        for n in range(SENT // 8):
            rows = spectrum[pl.ds(o + 8 * n, 8), :]
            if n < 3:
                rows = jnp.where(free, pltpu.roll(tail, 96 - 32 * n, 1), rows)
            out_ref[s, 8 * n : 8 * n + 8, :] = rows


def predict_kernel(k_ref, uv_ref, m_ref, rows_ref, coef_ref, res_ref, send_ref):
    uv = uv_ref[...].astype(F32)
    angles = half_turn(uv)
    iota = lax.broadcasted_iota(jnp.int32, (WIDTH, 128), 0)
    threes = iota % 3 == 0
    kap = iota.astype(F32)
    ar, ai, br, bi = (coef_ref[n] for n in range(4))
    zeros = jnp.zeros((128 - 2 * WIDTH, 128), F32)
    lane = lax.broadcasted_iota(jnp.int32, (8, 128), 1)

    def unpack(f):
        tail = pltpu.roll(k_ref[f, 0:8, :], 32, 1)
        for n in (1, 2):
            piece = pltpu.roll(k_ref[f, 8 * n : 8 * n + 8, :], 32 * n + 32, 1)
            tail = jnp.where(lane < 32 * n, tail, piece)
        return split(jnp.concatenate([k_ref[f], tail], axis=0))


    mixes, others = [], []
    for f in range(FACETS):
        cot = rows_ref[f]
        square = 1.0 + cot * cot
        pr, pi = [], []
        for n in range(2):
            cell = 3.0 * uv[n : n + 1] - float(f * WIDTH)
            value = cotangent(cot, square, angles[n : n + 1], kap, cell, threes)
            pr.append(ar + br * value)
            pi.append(ai + bi * value)
        left = jnp.concatenate([pr[0], -pi[0], zeros], axis=0)
        right = jnp.concatenate([pi[0], pr[0], zeros], axis=0)
        mixes.append(split(jnp.concatenate([left, right], axis=1)))
        others.append((pr[1], pi[1]))
    sums = [dot3(unpack(f), mixes[f]) for f in range(FACETS)]
    sr = jnp.zeros((WIDTH, 128), F32)
    si = jnp.zeros((WIDTH, 128), F32)
    for f in range(FACETS):
        tr, ti = sums[f][:, :128], sums[f][:, 128:]
        pr, pi = others[f]
        sr = sr + (tr * pr - ti * pi)
        si = si + (tr * pi + ti * pr)
    res = jnp.concatenate(
        [
            m_ref[0:1] - jnp.sum(sr, axis=0, keepdims=True) * (1.0 / SUBGRID),
            m_ref[1:2] - jnp.sum(si, axis=0, keepdims=True) * (1.0 / SUBGRID),
        ],
        axis=0,
    )
    res_ref[...] = res
    send_ref[...] = jnp.broadcast_to(
        jnp.concatenate([res, uv], axis=0)[None], (FACETS * COLS, 4, 128)
    )


def image_kernel(
    offset_hbm, got_ref, live_ref, gamma_ref, tw_ref, b_ref, out_hbm, grid, mid, out_ref, offset_ref, sem
):
    fetch = pltpu.make_async_copy(offset_hbm, offset_ref, sem.at[6])
    fetch.start()
    facet, column = lax.axis_index("facet"), lax.axis_index("col")
    grid[...] = jnp.zeros((3, PADDED, 2 * WIDTH), F32)
    iota = lax.broadcasted_iota(jnp.int32, (16, 128), 0)
    kap = (iota + 16 * facet).astype(F32)
    cot = live_ref[facet]
    square = 1.0 + cot * cot
    one_h = jnp.where(iota == 0, 1.0, 0.0).astype(BF16)
    none_h = jnp.zeros((32, 128), BF16)
    lanes = lax.broadcasted_iota(jnp.int32, (1, 2 * WIDTH), 1)
    turn = jnp.where(lanes < WIDTH, -1.0, 1.0)

    def swap(x):
        return turn * jnp.concatenate([x[:, WIDTH:], x[:, :WIDTH]], axis=1)


    def parts(angle, cell):
        hi, lo = split(ratio(cot, square, angle))
        hit = jnp.where(kap == cell, 1.0, 0.0).astype(BF16)
        return jnp.concatenate([hi, hit, one_h], axis=0), lo

    fetch.wait()

    def step(g, carry):
        first = g * (GROUP // FACETS)
        gots, turns = [], []
        for n in range(GROUP):
            got = got_ref[g * GROUP + n]
            angles = half_turn(got)
            gots.append([got[r : r + 1] for r in range(4)])
            turns.append([angles[r : r + 1] for r in (2, 3)])
        gs, vs, hs = {}, {}, {}

        def gamma(n):
            gam = gamma_ref[column, first + n // FACETS]
            return jnp.concatenate([gam, gam[:, :32]], axis=1)

        def rows_of(n):
            h, l = parts(turns[n][0], gots[n][2])
            gs[n] = dot(gamma(n), jnp.concatenate([h, h, l], axis=0))
            vs[n] = parts(turns[n][1], gots[n][3])

        def columns_of(n):
            rr, ri = gots[n][0], gots[n][1]
            gr, gi = gs[n][:WIDTH], gs[n][WIDTH:]
            w = jnp.concatenate([gr * rr - gi * ri, gr * ri + gi * rr], axis=0)
            wh, wl = split(w)
            vh, vl = vs[n]
            left = jnp.concatenate(
                [jnp.concatenate([vh, vh], axis=1), jnp.concatenate([vl, none_h], axis=1)], axis=0
            )
            hs[n] = dot(left, jnp.concatenate([wh, wl], axis=1), transposed=True)

        def place(n):
            h = hs[n]
            total = swap(h[WIDTH : WIDTH + 1])
            o = offset_ref[first + n // FACETS, n % FACETS]
            for m in range(3):
                add = h[16 * m : 16 * m + 16]
                if m < 2:
                    add = add + h[64 + 16 * m : 80 + 16 * m] + total
                at = pl.ds(o + (m + 1) % 3, 16, stride=3)
                grid[m, at, :] = grid[m, at, :] + add

        for n in range(GROUP + LAG2):
            for fn, lag in ((rows_of, 0), (columns_of, LAG1), (place, LAG2)):
                if 0 <= n - lag < GROUP:
                    fn(n - lag)
        return carry

    lax.fori_loop(0, FACETS * COLS // GROUP, step, 0)
    grid[:, 0:WIDTH, :] = grid[:, 0:WIDTH, :] + grid[:, LENGTH:PADDED, :]
    q = float(FACETS * WIDTH * WIDTH) ** (-0.25)
    for row in range(0, LENGTH, 64):
        one, two, nil = (grid[m, row : row + 64, :] for m in range(3))
        d = (SUBGRID * q) * nil + (q * math.sqrt(3) / 4) * (one - two)
        grid[2, row : row + 64, :] = d - (0.75 * q) * swap(one + two)
    right = (b_ref[0], b_ref[1])
    lefts = []
    for beta in range(16):
        d = grid[2, pl.ds(beta, 128, stride=16), :].T
        lefts.append(split(jnp.concatenate([d[0:WIDTH], d[WIDTH:]], axis=1)))
    freqs = [dot3(left, right) for left in lefts]
    for beta in range(16):
        yr, yi = freqs[beta][:, :128], freqs[beta][:, 128:]
        c = tw_ref[0, beta : beta + 1, :]
        s = tw_ref[1, beta : beta + 1, :]
        mid[beta, :, 0:128] = yr * c - yi * s
        mid[beta, :, 128:256] = yi * c + yr * s
    copies = []
    for r in range(0, WIDTH, 8):
        ys = fft_list(
            [(mid[b, r : r + 8, 0:128], mid[b, r : r + 8, 128:256]) for b in range(16)], 1.0
        )
        for t in range(16):
            out_ref[0, r : r + 8, 128 * t : 128 * t + 128] = ys[t][0]
            out_ref[1, r : r + 8, 128 * t : 128 * t + 128] = ys[t][1]
        rows = pl.ds(r, 8)
        copies.append(
            pltpu.make_async_copy(out_ref.at[:, rows, :], out_hbm.at[:, rows, :], sem.at[r // 8])
        )
        copies[-1].start()
    for copy in copies:
        copy.wait()


def keep(x):
    return pltpu.with_memory_space_constraint(x, pltpu.MemorySpace.HBM)


def params():
    return pltpu.CompilerParams(vmem_limit_bytes=48 << 20)


VM = pltpu.MemorySpace.VMEM


def solution(mesh):
    twiddle, forward, backward, rows, live, a, b = tables()
    coef = row_coefficients(a, b)
    gamma = image_rows(a, b)

    def body(strips, sub_offset, uv_cells, measured):
        vm = pl.BlockSpec(memory_space=VM)
        hbm = pl.BlockSpec(memory_space=pltpu.MemorySpace.HBM)
        windows = pl.pallas_call(
            extract_kernel,
            out_shape=jax.ShapeDtypeStruct((FACETS, SENT, 128), F32),
            in_specs=[hbm, hbm, hbm, hbm],
            out_specs=vm,
            scratch_shapes=[
                pltpu.VMEM((16, WIDTH, 256), F32),
                pltpu.VMEM((PADDED, 128), F32),
                pltpu.SMEM((COLS, FACETS), jnp.int32),
                pltpu.VMEM((2, WIDTH, LENGTH), F32),
                pltpu.VMEM((2, 16, 128), F32),
                pltpu.VMEM((2, 128, 256), BF16),
                pltpu.SemaphoreType.DMA((9,)),
            ],
            compiler_params=params(),
            name="extract",
        )(*(keep(x) for x in (sub_offset, strips[0], jnp.asarray(twiddle), jnp.asarray(forward))))
        arrived = lax.all_to_all(windows, "facet", split_axis=0, concat_axis=0, tiled=True)
        res, send = pl.pallas_call(
            predict_kernel,
            out_shape=(
                jax.ShapeDtypeStruct((2, 128), F32),
                jax.ShapeDtypeStruct((FACETS * COLS, 4, 128), F32),
            ),
            in_specs=[vm] * 5,
            out_specs=(vm, vm),
            compiler_params=params(),
            name="predict",
        )(arrived, uv_cells[0, 0], measured[0, 0], jnp.asarray(rows), jnp.asarray(coef))
        got = lax.all_to_all(send, ("col", "facet"), split_axis=0, concat_axis=0, tiled=True)
        image = pl.pallas_call(
            image_kernel,
            out_shape=jax.ShapeDtypeStruct((2, WIDTH, LENGTH), F32),
            in_specs=[hbm, vm, vm, vm, vm, vm],
            out_specs=pl.BlockSpec(memory_space=pl.ANY),
            scratch_shapes=[
                pltpu.VMEM((3, PADDED, 2 * WIDTH), F32),
                pltpu.VMEM((16, WIDTH, 256), F32),
                pltpu.VMEM((2, WIDTH, LENGTH), F32),
                pltpu.SMEM((COLS, FACETS), jnp.int32),
                pltpu.SemaphoreType.DMA((7,)),
            ],
            compiler_params=params(),
            name="image",
        )(
            keep(sub_offset),
            got,
            jnp.asarray(live),
            jnp.asarray(gamma),
            jnp.asarray(twiddle),
            jnp.asarray(backward),
        )
        return image[None], res[None, None]

    return jax.shard_map(
        body,
        mesh=mesh,
        in_specs=(
            P("facet", None, "col", None),
            P(),
            P("col", "facet", None, None),
            P("col", "facet", None, None),
        ),
        out_specs=(P("facet", None, "col", None), P("col", "facet", None, None)),
        check_vma=False,
    )
```
